32 devices in a mesh: section: 4 (over z), dp: 8 (over y, x, core).
Axes of the slice: x: 2, y: 2, z: 4, core: 2. Of those that a mesh axis runs over, the one named last changes fastest.
Arguments:
- images: bfloat16 [2, 8, 576, 768], P(None, 'dp'), may hold values from -6 to 6
- cotangent: bfloat16 [2, 8, 576, 768], P(None, 'dp'), may hold values from -6 to 6
- groups: int32 [2, 8], P(None, 'dp'), may hold values from 0 to 1
- norm_gain: float32 [4, 2, 768], P('section'), may hold values from 0.5 to 1.5
- norm_bias: float32 [4, 2, 768], P('section'), may hold values from -2 to 2
- small_in: bfloat16 [4, 196, 384], P('section', None, 'dp'), may hold values from -0.4375 to 0.4375
- small_out: bfloat16 [4, 384, 196], P('section', 'dp'), may hold values from -0.3125 to 0.3125
- large_in: bfloat16 [4, 576, 384], P('section', None, 'dp'), may hold values from -0.25 to 0.25
- large_out: bfloat16 [4, 384, 576], P('section', 'dp'), may hold values from -0.3125 to 0.3125
- token_bias: float32 [4, 2, 384], P('section'), may hold values from -3 to 3
- small_patch_bias: float32 [4, 196], P('section'), may hold values from -3 to 3
- large_patch_bias: float32 [4, 576], P('section'), may hold values from -3 to 3
- channel_in: bfloat16 [4, 768, 3072], P('section', None, 'dp'), may hold values from -0.21875 to 0.21875
- channel_out: bfloat16 [4, 3072, 768], P('section', 'dp'), may hold values from -0.109375 to 0.109375
- channel_bias: float32 [4, 3840], P('section'), may hold values from -3 to 3
Outputs:
- section_outputs: bfloat16 [4, 2, 8, 576, 768], P('section', None, 'dp')
- section_grads: bfloat16 [4, 2, 8, 576, 768], P('section', None, 'dp')
- grad_norm_gain: float32 [4, 2, 768], P('section')
- grad_norm_bias: float32 [4, 2, 768], P('section')
- grad_small_in: float32 [4, 196, 384], P('section', None, 'dp')
- grad_small_out: float32 [4, 384, 196], P('section', 'dp')
- grad_large_in: float32 [4, 576, 384], P('section', None, 'dp')
- grad_large_out: float32 [4, 384, 576], P('section', 'dp')
- grad_token_bias: float32 [4, 2, 384], P('section')
- grad_small_patch_bias: float32 [4, 196], P('section')
- grad_large_patch_bias: float32 [4, 576], P('section')
- grad_channel_in: float32 [4, 768, 3072], P('section', None, 'dp')
- grad_channel_out: float32 [4, 3072, 768], P('section', 'dp')
- grad_channel_bias: float32 [4, 3840], P('section')
The draws below stay inside these ranges and needn't reach their ends.
Inputs may be any that keep to these rules, and one draw needn't show every extreme that they name: `groups`: 1 marks a slot holding one image of 576 patches, 0 a slot whose first 392 rows hold two images of 196 patches.
All inputs are finite; a program needn't handle non-finite values.
Results may differ from the reference program's by a relative error of at most 0.019.
Values may be sent and summed in bfloat16 or wider, within the bound.
No kernel may reach another device: no remote copies, remote signals or barrier semaphores. Data moves between devices by JAX's collectives and lax.ppermute only.
A program may use at most 256 MiB of HBM per device.

```python
import jax
import jax.numpy as jnp
from jax import lax

D = 768
CH = 3072
TH = 384
PS = 196
PL = 576
MB = 2
SLOTS = 8
N_SECTION = 4


def touch_ends(array, rng, low, high):
    place = [jax.random.randint(jax.random.fold_in(rng, axis), (), 0, length) for axis, length in enumerate(array.shape)]
    widest = array.shape.index(max(array.shape))
    neighbour = place[:widest] + [(place[widest] + 1) % array.shape[widest]] + place[widest + 1:]
    return array.at[tuple(place)].set(low).at[tuple(neighbour)].set(high)


def shard_levels(own_key, dims, cuts, low, largest):
    def one(dim, parts):
        draws = jax.random.uniform(jax.random.fold_in(jax.random.fold_in(own_key, 6), dim), (parts,), jnp.float32, low / len(cuts), largest / len(cuts))
        return jnp.repeat(jnp.exp(draws), dims[dim] // parts).reshape((-1,) + (1,) * (len(dims) - dim - 1))

    factor_of = one(*cuts[0])
    for cut in cuts[1:]:
        factor_of = factor_of * one(*cut)
    return factor_of


def normal_values(own_key, extent, width, most, cuts=(), held_as=jnp.bfloat16):
    drawn = jax.random.normal(own_key, extent, jnp.float32) * width
    if len(cuts) > 0:
        drawn = shard_levels(own_key, extent, cuts, -0.22, 0.18) * drawn
    return jnp.clip(drawn, min=-most, max=most).astype(held_as)


def setup_inputs(seed: int = 0) -> dict:
    splits = jax.random.split(jax.random.key(seed), 16)
    images = normal_values(splits[0], (MB, SLOTS, PL, D), 1.0, 6.0, ((1, 8),))
    cotangent = normal_values(splits[1], (MB, SLOTS, PL, D), 1.0, 6.0, ((1, 8),))
    groups = touch_ends(jax.random.randint(splits[2], (MB, SLOTS), 0, 2), jax.random.fold_in(splits[2], 1), 0, 1).astype(jnp.int32)
    norm_gain = jnp.clip(1.0 + 0.1 * jax.random.normal(splits[3], (N_SECTION, 2, D), jnp.float32), 0.5, 1.5)
    norm_bias = normal_values(splits[4], (N_SECTION, 2, D), 0.3, 2.0, ((0, 4),), jnp.float32)
    small_in = normal_values(splits[5], (N_SECTION, PS, TH), PS ** -0.5, 0.4375, ((0, 4), (2, 8)))
    small_out = normal_values(splits[6], (N_SECTION, TH, PS), TH ** -0.5, 0.3125, ((0, 4), (1, 8)))
    large_in = normal_values(splits[7], (N_SECTION, PL, TH), PL ** -0.5, 0.25, ((0, 4), (2, 8)))
    large_out = normal_values(splits[8], (N_SECTION, TH, PL), TH ** -0.5, 0.3125, ((0, 4), (1, 8)))
    token_bias = normal_values(splits[9], (N_SECTION, 2, TH), 0.5, 3.0, ((0, 4),), jnp.float32)
    small_patch_bias = normal_values(splits[10], (N_SECTION, PS), 0.5, 3.0, ((0, 4),), jnp.float32)
    large_patch_bias = normal_values(splits[11], (N_SECTION, PL), 0.5, 3.0, ((0, 4),), jnp.float32)
    channel_in = normal_values(splits[12], (N_SECTION, D, CH), D ** -0.5, 0.21875, ((0, 4), (2, 8)))
    channel_out = normal_values(splits[13], (N_SECTION, CH, D), CH ** -0.5, 0.109375, ((0, 4), (1, 8)))
    channel_bias = normal_values(splits[14], (N_SECTION, CH + D), 0.5, 3.0, ((0, 4),), jnp.float32)
    return {"images": images, "cotangent": cotangent, "groups": groups, "norm_gain": norm_gain, "norm_bias": norm_bias, "small_in": small_in, "small_out": small_out, "large_in": large_in, "large_out": large_out, "token_bias": token_bias, "small_patch_bias": small_patch_bias, "large_patch_bias": large_patch_bias, "channel_in": channel_in, "channel_out": channel_out, "channel_bias": channel_bias}


EPSILON = 1e-06
HIGHEST = lax.Precision.HIGHEST

@jax.custom_vjp
def low(v):
    return lax.optimization_barrier(v.astype(jnp.bfloat16)).astype(jnp.float32)

@jax.custom_vjp
def low_back(v):
    return v

def low_keep(v):
    return (low(v), None)

def low_pass(kept, grad):
    return (grad,)

def back_keep(v):
    return (v, None)

def back_low(kept, grad):
    return (low(grad),)
low.defvjp(low_keep, low_pass)
low_back.defvjp(back_keep, back_low)

def layer_norm(values, scale_row, shift_row):
    row_mean = lax.optimization_barrier(jnp.mean(values, axis=-1, keepdims=True))
    centred = values - row_mean
    spread = lax.optimization_barrier(jnp.mean(centred * centred, axis=-1, keepdims=True))
    return centred * lax.rsqrt(spread + EPSILON) * scale_row + shift_row

def gelu_tanh(values):
    return jax.nn.gelu(values, approximate=True)

def mixer_block(images, norm_gains, norm_shifts, token_first, token_hidden, token_second, token_patch, chan_first, chan_hidden, chan_second, chan_output):
    normed = low(layer_norm(images, norm_gains[0], norm_shifts[0]))
    hidden_pre = low_back(jnp.einsum('bpd,ph->bdh', normed, token_first, precision=HIGHEST) + token_hidden)
    hidden = low(gelu_tanh(hidden_pre))
    mixed_out = low_back(jnp.einsum('bdh,hp->bpd', hidden, token_second, precision=HIGHEST) + token_patch[None, :, None])
    middle = images + mixed_out
    normed_two = low(layer_norm(middle, norm_gains[1], norm_shifts[1]))
    inner_pre = low_back(jnp.einsum('bpd,de->bpe', normed_two, chan_first, precision=HIGHEST) + chan_hidden)
    inner_act = low(gelu_tanh(inner_pre))
    branch = low_back(jnp.einsum('bpe,ed->bpd', inner_act, chan_second, precision=HIGHEST) + chan_output)
    return middle + branch

def section_layer(entry, group, weights):
    gain_rows, bias_rows, small_first, small_second, large_first, large_second, token_rows, small_patch, large_patch, chan_first, chan_second, chan_bias = weights
    chan_hidden = chan_bias[:CH]
    chan_output = chan_bias[CH:]

    def run_large(values):
        result = mixer_block(values[None], gain_rows, bias_rows, large_first, token_rows[1], large_second, large_patch, chan_first, chan_hidden, chan_second, chan_output)
        return result[0]

    def run_small(values):
        pieces = values[:2 * PS].reshape(2, PS, D)
        result = mixer_block(pieces, gain_rows, bias_rows, small_first, token_rows[0], small_second, small_patch, chan_first, chan_hidden, chan_second, chan_output)
        return jnp.concatenate([result.reshape(2 * PS, D), jnp.zeros((PL - 2 * PS, D), jnp.float32)], axis=0)
    return lax.cond(group == 1, run_large, run_small, entry)

def run_slot(params, slot_input, slot_perturb, group):
    previous = slot_input
    results = []
    for section_number in range(N_SECTION):
        entry = low_back(previous + slot_perturb[section_number])
        weights = tuple((w[section_number] for w in params))
        previous = low(section_layer(entry, group, weights))
        results.append(previous)
    return jnp.stack(results)

def reference(images, cotangent, groups, norm_gain, norm_bias, small_in, small_out, large_in, large_out, token_bias, small_patch_bias, large_patch_bias, channel_in, channel_out, channel_bias):
    params = tuple((w.astype(jnp.float32) for w in (norm_gain, norm_bias, small_in, small_out, large_in, large_out, token_bias, small_patch_bias, large_patch_bias, channel_in, channel_out, channel_bias)))
    slot_count = MB * SLOTS
    inputs = images.astype(jnp.float32).reshape(slot_count, PL, D)
    flat_groups = groups.reshape(slot_count).astype(jnp.int32)
    perturb = jnp.zeros((slot_count, N_SECTION, PL, D), jnp.float32)
    checked = jax.checkpoint(run_slot)

    def forward(weights, perturbs):

        def one_slot(item):
            return checked(weights, item[0], item[1], item[2])
        return lax.map(one_slot, (inputs, perturbs, flat_groups))
    outputs, pullback = jax.vjp(forward, params, perturb)
    output_grads = jnp.zeros_like(outputs).at[:, N_SECTION - 1].set(cotangent.astype(jnp.float32).reshape(slot_count, PL, D))
    weight_grads, entry_grads = pullback(output_grads)
    section_outputs = outputs.reshape(MB, SLOTS, N_SECTION, PL, D).transpose(2, 0, 1, 3, 4).astype(jnp.bfloat16)
    section_grads = entry_grads.reshape(MB, SLOTS, N_SECTION, PL, D).transpose(2, 0, 1, 3, 4).astype(jnp.bfloat16)
    return (section_outputs, section_grads, weight_grads[0], weight_grads[1], weight_grads[2], weight_grads[3], weight_grads[4], weight_grads[5], weight_grads[6], weight_grads[7], weight_grads[8], weight_grads[9], weight_grads[10], weight_grads[11])
```

```python
import functools

import jax
import jax.numpy as jnp
from jax import lax
from jax.experimental import pallas as pl
from jax.experimental.pallas import tpu as pltpu
from jax.sharding import PartitionSpec as P

EPSILON = 1e-06
F32 = jnp.float32
BF16 = jnp.bfloat16
ROOT = 0.7978845608028654
CUBE = 0.044715
PIECES = 8
PAIRS = 4
CHUNK = 64
VMEM_LIMIT = 44 * 2**20

WHOLE = pl.BlockSpec(memory_space=pltpu.VMEM)
SCALARS = pl.BlockSpec(memory_space=pltpu.SMEM)
ANYWHERE = pl.BlockSpec(memory_space=pl.ANY)


def nn(a, b):
    return jnp.dot(a, b, preferred_element_type=F32)


def nt(a, b):
    return lax.dot_general(a, b, (((1,), (1,)), ((), ())), preferred_element_type=F32)


def tn(a, b):
    return lax.dot_general(a, b, (((0,), (0,)), ((), ())), preferred_element_type=F32)


def gelu_and_slope(v):
    square = v * v
    t = jnp.tanh(v * (ROOT + (ROOT * CUBE) * square))
    half = 0.5 * (1.0 + t)
    slope = half + (0.5 * v) * (1.0 - t * t) * (ROOT + (3.0 * ROOT * CUBE) * square)
    return v * half, slope


def centre(v):
    c = v - jnp.mean(v, axis=-1, keepdims=True)
    r = lax.rsqrt(jnp.mean(c * c, axis=-1, keepdims=True) + EPSILON)
    return c * r, r


def norm_back(grad, xhat, rstd, gain):
    g = grad * gain
    m1 = jnp.mean(g, axis=-1, keepdims=True)
    m2 = jnp.mean(g * xhat, axis=-1, keepdims=True)
    return rstd * (g - m1 - xhat * m2)


def fold(v):
    return v.reshape(v.shape[0] // 8, 8, v.shape[1]).sum(axis=0)


def piece_number(r):
    return ((r >> 2) & 1) | ((r & 1) << 1) | (((r >> 1) & 1) << 2)


class Sizes:
    def __init__(self, rows, small, width, tokens, hidden):
        self.rows, self.small, self.width, self.tokens, self.hidden = rows, small, width, tokens, hidden
        self.large_pad = -(-rows // 128) * 128
        self.small_pad = -(-small // 128) * 128
        self.pack = 2 * (self.large_pad + self.small_pad)
        self.c_l1, self.c_l2 = 0, self.large_pad
        self.c_s1 = 2 * self.large_pad
        self.c_s2 = self.c_s1 + self.small_pad
        self.bias_col = rows
        self.block = hidden // PIECES
        self.pair = hidden // PAIRS


def token_forward_kernel(z, sc, x_ref, t_ref, v_ref, m_ref, c_ref, a_ref, g_ref, s_ref, af_ref):
    live, kind = sc[0], sc[1]

    @pl.when(live == 1)
    def _():
        gain1, gain2, shift1, shift2 = v_ref[0:1, :], v_ref[1:2, :], v_ref[2:3, :], v_ref[3:4, :]

        def first(i, _):
            at = pl.ds(pl.multiple_of(i * CHUNK, CHUNK), CHUNK)
            xhat, _r = centre(x_ref[at, :].astype(F32))
            a = xhat * gain1 + shift1
            af_ref[at, :] = a
            a_ref[at, :] = a.astype(BF16)
            return 0

        lax.fori_loop(0, z.rows // CHUNK, first, 0)
        columns = v_ref[0:8, :].T

        @pl.when(kind == 1)
        def _():
            w1 = t_ref[:, z.c_l1 : z.c_l1 + z.rows]
            b = [t_ref[:, z.bias_col + k : z.bias_col + k + 1].astype(F32) for k in range(3)]
            pre = nn(w1, a_ref[...]) + (b[0] + b[1] + b[2])
            g, s = gelu_and_slope(pre)
            g = g.astype(BF16)
            g_ref[0 : z.tokens, :] = g
            s_ref[0 : z.tokens, :] = s.astype(BF16)
            w2 = t_ref[:, z.c_l2 : z.c_l2 + z.rows]
            m_ref[...] = x_ref[...].astype(F32) + (tn(w2, g) + columns[0 : z.rows, 5:6])

        @pl.when(kind == 0)
        def _():
            w1 = t_ref[:, z.c_s1 : z.c_s1 + z.small_pad]
            w2 = t_ref[:, z.c_s2 : z.c_s2 + z.small_pad]
            b = [t_ref[:, z.bias_col + 3 + k : z.bias_col + 4 + k].astype(F32) for k in range(3)]
            m_ref[...] = x_ref[...].astype(F32)
            for image in range(2):
                lo = image * z.small
                a = af_ref[lo : lo + z.small_pad, :].astype(BF16)
                pre = nn(w1, a) + (b[0] + b[1] + b[2])
                g, s = gelu_and_slope(pre)
                g = g.astype(BF16)
                g_ref[image * z.tokens : (image + 1) * z.tokens, :] = g
                s_ref[image * z.tokens : (image + 1) * z.tokens, :] = s.astype(BF16)
                mixed = tn(w2, g) + columns[0 : z.small_pad, 6:7]
                m_ref[lo : lo + z.small, :] = m_ref[lo : lo + z.small, :] + mixed[0 : z.small, :]

        def second(i, _):
            at = pl.ds(pl.multiple_of(i * CHUNK, CHUNK), CHUNK)
            xhat, _r = centre(m_ref[at, :])
            c_ref[at, :] = (xhat * gain2 + shift2).astype(BF16)
            return 0

        lax.fori_loop(0, z.rows // CHUNK, second, 0)


def token_forward(z, sc, x, pack, v):
    sds = jax.ShapeDtypeStruct
    return pl.pallas_call(
        functools.partial(token_forward_kernel, z),
        in_specs=[SCALARS, WHOLE, WHOLE, WHOLE],
        out_specs=[WHOLE] * 5,
        out_shape=[
            sds((z.rows, z.width), F32),
            sds((z.rows, z.width), BF16),
            sds((z.rows, z.width), BF16),
            sds((2 * z.tokens, z.width), BF16),
            sds((2 * z.tokens, z.width), BF16),
        ],
        scratch_shapes=[pltpu.VMEM((z.rows, z.width), F32)],
        compiler_params=pltpu.CompilerParams(vmem_limit_bytes=VMEM_LIMIT),
        cost_estimate=pl.CostEstimate(flops=700_000_000, transcendentals=300_000, bytes_accessed=10_000_000),
    )(sc, x, pack, v)


def piece_refs(refs, second_way):
    own, one, stack, core_first, core_stack = refs
    if second_way:
        half = [own, stack.at[0], one, stack.at[1], core_first.at[0], core_stack.at[0], core_first.at[1], core_stack.at[1]]
    else:
        half = [own, one, stack.at[0], stack.at[1], core_first.at[0], core_first.at[1], core_stack.at[0], core_stack.at[1]]
    return half


def load_pair(z, sets, select, j, slot, ci_buf, co_buf, sem):
    def go(ci_refs, co_refs):
        for k in range(PAIRS):

            @pl.when(j == k)
            def _():
                for h in range(2):
                    part = pl.ds(h * z.block, z.block)
                    pltpu.make_async_copy(ci_refs[2 * k + h], ci_buf.at[slot, :, part], sem.at[slot, h]).start()
                    pltpu.make_async_copy(co_refs[2 * k + h], co_buf.at[slot, part, :], sem.at[slot, 2 + h]).start()

    if len(sets) == 1:
        go(*sets[0])
    else:
        for n, one in enumerate(sets):
            pl.when(select == n)(functools.partial(go, *one))


def wait_pair(z, sets, slot, ci_buf, co_buf, sem):
    ci_refs, co_refs = sets[0]
    for h in range(2):
        part = pl.ds(h * z.block, z.block)
        pltpu.make_async_copy(ci_refs[0], ci_buf.at[slot, :, part], sem.at[slot, h]).wait()
        pltpu.make_async_copy(co_refs[0], co_buf.at[slot, part, :], sem.at[slot, 2 + h]).wait()


def weight_sets(refs):
    return [
        (piece_refs(refs[10 * n : 10 * n + 5], False), piece_refs(refs[10 * n + 5 : 10 * n + 10], True))
        for n in range(len(refs) // 10)
    ]


def pair_bias(z, v_ref, dp, j):
    rows = [8 + (dp ^ piece_number(2 * j + h)) for h in range(2)]
    return jnp.concatenate([v_ref[pl.ds(r, 1), 0 : z.block] for r in rows], axis=1)


def channel_forward_kernel(z, n_sets, sc, c_ref, m_ref, v_ref, *refs):
    weights = weight_sets(refs[: 10 * n_sets])
    out_ref, r_hbm, s_hbm, acc, ci_buf, co_buf, r_buf, s_buf, sem, out_sem = refs[10 * n_sets :]
    live, kind, dp, select = sc[0], sc[1], sc[2], sc[3]
    parts = 4
    rows = z.rows // parts

    @pl.when(live == 1)
    def _():
        load_pair(z, weights, select, 0, 0, ci_buf, co_buf, sem)
        acc[...] = m_ref[...] + v_ref[4:5, :]

        def step(j, _):
            slot = lax.rem(j, 2)
            wait_pair(z, weights, slot, ci_buf, co_buf, sem)

            @pl.when(j + 1 < PAIRS)
            def _():
                load_pair(z, weights, select, j + 1, 1 - slot, ci_buf, co_buf, sem)

            @pl.when(j >= 2)
            def _():
                pltpu.make_async_copy(r_buf.at[slot], r_hbm.at[0], out_sem.at[slot, 0]).wait()
                pltpu.make_async_copy(s_buf.at[slot], s_hbm.at[0], out_sem.at[slot, 1]).wait()

            bias = pair_bias(z, v_ref, dp, j)
            for i in range(parts):
                at = pl.ds(i * rows, rows)
                g, s = gelu_and_slope(nn(c_ref[at, :], ci_buf[slot]) + bias)
                g = g.astype(BF16)
                r_buf[slot, at, :] = g
                s_buf[slot, at, :] = s.astype(BF16)
                acc[at, :] += nn(g, co_buf[slot])
            pltpu.make_async_copy(r_buf.at[slot], r_hbm.at[j], out_sem.at[slot, 0]).start()
            pltpu.make_async_copy(s_buf.at[slot], s_hbm.at[j], out_sem.at[slot, 1]).start()
            return 0

        lax.fori_loop(0, PAIRS, step, 0)
        used = lax.broadcasted_iota(jnp.int32, (z.rows, 1), 0) < jnp.where(kind == 1, z.rows, 2 * z.small)
        out_ref[...] = jnp.where(used, acc[...], 0.0).astype(BF16)
        for slot in range(2):
            pltpu.make_async_copy(r_buf.at[slot], r_hbm.at[0], out_sem.at[slot, 0]).wait()
            pltpu.make_async_copy(s_buf.at[slot], s_hbm.at[0], out_sem.at[slot, 1]).wait()


def channel_forward(z, sc, c, m, v, sets):
    sds = jax.ShapeDtypeStruct
    flat = [a for one in sets for a in one]
    return pl.pallas_call(
        functools.partial(channel_forward_kernel, z, len(sets)),
        in_specs=[SCALARS, WHOLE, WHOLE, WHOLE] + [ANYWHERE] * len(flat),
        out_specs=[WHOLE, ANYWHERE, ANYWHERE],
        out_shape=[
            sds((z.rows, z.width), BF16),
            sds((PAIRS, z.rows, z.pair), BF16),
            sds((PAIRS, z.rows, z.pair), BF16),
        ],
        scratch_shapes=[
            pltpu.VMEM((z.rows, z.width), F32),
            pltpu.VMEM((2, z.width, z.pair), BF16),
            pltpu.VMEM((2, z.pair, z.width), BF16),
            pltpu.VMEM((2, z.rows, z.pair), BF16),
            pltpu.VMEM((2, z.rows, z.pair), BF16),
            pltpu.SemaphoreType.DMA((2, 4)),
            pltpu.SemaphoreType.DMA((2, 2)),
        ],
        compiler_params=pltpu.CompilerParams(vmem_limit_bytes=VMEM_LIMIT),
        cost_estimate=pl.CostEstimate(flops=5_400_000_000, transcendentals=1_800_000, bytes_accessed=20_000_000),
    )(sc, c, m, v, *flat)


def channel_backward_kernel(z, n_sets, sc, dy_ref, s_hbm, m_ref, v_ref, *refs):
    weights = weight_sets(refs[: 10 * n_sets])
    dm_ref, dq_hbm, dv_ref, dh_ref, acc, ci_buf, co_buf, s_buf, q_buf, sem, s_sem, out_sem = refs[10 * n_sets :]
    live, dp, select = sc[0], sc[2], sc[3]
    parts = 4
    rows = z.rows // parts

    @pl.when(live == 1)
    def _():
        load_pair(z, weights, select, 0, 0, ci_buf, co_buf, sem)
        pltpu.make_async_copy(s_hbm.at[0], s_buf.at[0], s_sem.at[0]).start()

        def step(j, _):
            slot = lax.rem(j, 2)
            wait_pair(z, weights, slot, ci_buf, co_buf, sem)
            pltpu.make_async_copy(s_hbm.at[0], s_buf.at[slot], s_sem.at[slot]).wait()

            @pl.when(j + 1 < PAIRS)
            def _():
                load_pair(z, weights, select, j + 1, 1 - slot, ci_buf, co_buf, sem)
                pltpu.make_async_copy(s_hbm.at[j + 1], s_buf.at[1 - slot], s_sem.at[1 - slot]).start()

            @pl.when(j >= 2)
            def _():
                pltpu.make_async_copy(q_buf.at[slot], dq_hbm.at[0], out_sem.at[slot]).wait()

            total = jnp.zeros((8, z.pair), F32)
            for i in range(parts):
                at = pl.ds(i * rows, rows)
                dq = nt(dy_ref[at, :], co_buf[slot]) * s_buf[slot, at, :].astype(F32)
                total = total + fold(dq)
                dq = dq.astype(BF16)
                q_buf[slot, at, :] = dq
                dc = nt(dq, ci_buf[slot])

                @pl.when(j == 0)
                def _():
                    acc[at, :] = dc

                @pl.when(j > 0)
                def _():
                    acc[at, :] += dc

            line = total.sum(axis=0, keepdims=True)
            for h in range(2):
                dh_ref[pl.ds(dp ^ piece_number(2 * j + h), 1), :] = line[:, h * z.block : (h + 1) * z.block]
            pltpu.make_async_copy(q_buf.at[slot], dq_hbm.at[j], out_sem.at[slot]).start()
            return 0

        lax.fori_loop(0, PAIRS, step, 0)
        gain2 = v_ref[1:2, :]

        def back(i, carry):
            dgain, dshift, dout = carry
            at = pl.ds(pl.multiple_of(i * CHUNK, CHUNK), CHUNK)
            xhat, rstd = centre(m_ref[at, :])
            dc = acc[at, :]
            dy = dy_ref[at, :].astype(F32)
            dm_ref[at, :] = dy + norm_back(dc, xhat, rstd, gain2)
            return (dgain + fold(dc * xhat), dshift + fold(dc), dout + fold(dy))

        zero = jnp.zeros((8, z.width), F32)
        sums = lax.fori_loop(0, z.rows // CHUNK, back, (zero, zero, zero))
        dv_ref[...] = jnp.zeros_like(dv_ref)
        for row, total in zip((1, 3, 4), sums):
            dv_ref[row : row + 1, :] = total.sum(axis=0, keepdims=True)
        for slot in range(2):
            pltpu.make_async_copy(q_buf.at[slot], dq_hbm.at[0], out_sem.at[slot]).wait()


def channel_backward(z, sc, dy, slope, m, v, sets):
    sds = jax.ShapeDtypeStruct
    flat = [a for one in sets for a in one]
    return pl.pallas_call(
        functools.partial(channel_backward_kernel, z, len(sets)),
        in_specs=[SCALARS, WHOLE, ANYWHERE, WHOLE, WHOLE] + [ANYWHERE] * len(flat),
        out_specs=[WHOLE, ANYWHERE, WHOLE, WHOLE],
        out_shape=[
            sds((z.rows, z.width), F32),
            sds((PAIRS, z.rows, z.pair), BF16),
            sds((8, z.width), F32),
            sds((8, z.block), F32),
        ],
        scratch_shapes=[
            pltpu.VMEM((z.rows, z.width), F32),
            pltpu.VMEM((2, z.width, z.pair), BF16),
            pltpu.VMEM((2, z.pair, z.width), BF16),
            pltpu.VMEM((2, z.rows, z.pair), BF16),
            pltpu.VMEM((2, z.rows, z.pair), BF16),
            pltpu.SemaphoreType.DMA((2, 4)),
            pltpu.SemaphoreType.DMA((2,)),
            pltpu.SemaphoreType.DMA((2,)),
        ],
        compiler_params=pltpu.CompilerParams(vmem_limit_bytes=VMEM_LIMIT),
        cost_estimate=pl.CostEstimate(flops=5_400_000_000, transcendentals=0, bytes_accessed=20_000_000),
    )(sc, dy, slope, m, v, *flat)


def token_backward_kernel(z, add, sc, dm_ref, x_ref, a_ref, t_ref, g_ref, s_ref, v_ref, *refs):
    prev_ref = refs[0]
    dx_ref, dt_ref, dv_ref, db_ref, da, dvb = refs[1:]
    live, kind = sc[0], sc[1]

    @pl.when(live == 1)
    def _():
        ones = jnp.ones((8, z.width), BF16)
        dvb[...] = dm_ref[...].astype(BF16)
        dv_ref[...] = jnp.zeros_like(dv_ref)
        by_patch = nt(ones, dvb[...])[0:1, :]
        db_ref[...] = jnp.zeros_like(db_ref)

        def put(lo, value):
            hi = lo + value.shape[1]
            if add:
                value = value + prev_ref[:, lo:hi].astype(F32)
            dt_ref[:, lo:hi] = value.astype(BF16)

        def keep(lo, n):
            dt_ref[:, lo : lo + n] = prev_ref[:, lo : lo + n] if add else jnp.zeros((z.tokens, n), BF16)

        @pl.when(kind == 1)
        def _():
            dv_ref[5:6, 0 : z.rows] = by_patch
            w1 = t_ref[:, z.c_l1 : z.c_l1 + z.rows]
            w2 = t_ref[:, z.c_l2 : z.c_l2 + z.rows]
            dz = (nn(w2, dvb[...]) * s_ref[0 : z.tokens, :].astype(F32)).astype(BF16)
            da[...] = tn(w1, dz)
            put(z.c_l1, nt(dz, a_ref[...]))
            put(z.c_l2, nt(g_ref[0 : z.tokens, :], dvb[...]))
            keep(z.c_s1, 2 * z.small_pad)
            db_ref[1:2, :] = nt(ones, dz)[0:1, :]

        @pl.when(kind == 0)
        def _():
            dv_ref[6:7, 0 : z.rows] = by_patch
            w1 = t_ref[:, z.c_s1 : z.c_s1 + z.small_pad]
            w2 = t_ref[:, z.c_s2 : z.c_s2 + z.small_pad]
            keep(z.c_l1, z.large_pad)
            keep(z.c_l2, z.large_pad)
            da[...] = a_ref[...].astype(F32)
            normed = [da[k * z.small : k * z.small + z.small_pad, :].astype(BF16) for k in range(2)]
            da[...] = jnp.zeros_like(da)
            dw1 = dw2 = dbias = 0.0
            for image in range(2):
                lo = image * z.small
                own = slice(image * z.tokens, (image + 1) * z.tokens)
                dv = dm_ref[lo : lo + z.small_pad, :].astype(BF16)
                dz = (nn(w2, dv) * s_ref[own, :].astype(F32)).astype(BF16)
                da[lo : lo + z.small, :] = tn(w1, dz)[0 : z.small, :]
                dw1 = dw1 + nt(dz, normed[image])
                dw2 = dw2 + nt(g_ref[own, :], dv)
                dbias = dbias + nt(ones, dz)[0:1, :]
            put(z.c_s1, dw1)
            put(z.c_s2, dw2)
            db_ref[0:1, :] = dbias

        gain1 = v_ref[0:1, :]

        def back(i, carry):
            dgain, dshift = carry
            at = pl.ds(pl.multiple_of(i * CHUNK, CHUNK), CHUNK)
            xhat, rstd = centre(x_ref[at, :].astype(F32))
            g = da[at, :]
            dx_ref[at, :] = (dm_ref[at, :] + norm_back(g, xhat, rstd, gain1)).astype(BF16)
            return (dgain + fold(g * xhat), dshift + fold(g))

        zero = jnp.zeros((8, z.width), F32)
        sums = lax.fori_loop(0, z.rows // CHUNK, back, (zero, zero))
        for row, total in zip((0, 2), sums):
            dv_ref[row : row + 1, :] = total.sum(axis=0, keepdims=True)


def token_backward(z, sc, dm, x, a, pack, g, s, v, prev, add):
    sds = jax.ShapeDtypeStruct
    return pl.pallas_call(
        functools.partial(token_backward_kernel, z, add),
        in_specs=[SCALARS] + [WHOLE] * 8,
        out_specs=[WHOLE] * 4,
        out_shape=[
            sds((z.rows, z.width), BF16),
            sds((z.tokens, z.pack), BF16),
            sds((8, z.width), F32),
            sds((8, z.tokens), F32),
        ],
        scratch_shapes=[pltpu.VMEM((z.rows, z.width), F32), pltpu.VMEM((z.rows, z.width), BF16)],
        input_output_aliases={8: 1},
        compiler_params=pltpu.CompilerParams(vmem_limit_bytes=VMEM_LIMIT),
        cost_estimate=pl.CostEstimate(flops=1_400_000_000, transcendentals=0, bytes_accessed=12_000_000),
    )(sc, dm, x, a, pack, g, s, v, prev)


def weight_grad_kernel(z, add, sc, c_ref, dy_ref, r_hbm, q_hbm, *refs):
    prev = refs[:4]
    ck, cs, ok, os_, ct, st, r_buf, q_buf, oc, oo, pc, po, in_sem, out_sem, prev_sem = refs[4:]
    live = sc[0]

    def fetch(j, slot):
        pltpu.make_async_copy(r_hbm.at[j], r_buf.at[slot], in_sem.at[slot, 0]).start()
        pltpu.make_async_copy(q_hbm.at[j], q_buf.at[slot], in_sem.at[slot, 1]).start()

    def arrived(slot):
        pltpu.make_async_copy(r_hbm.at[0], r_buf.at[slot], in_sem.at[slot, 0]).wait()
        pltpu.make_async_copy(q_hbm.at[0], q_buf.at[slot], in_sem.at[slot, 1]).wait()

    def moves(first, second, j, slot, out, sems):
        for h in range(2):
            part = pl.ds(h * z.block, z.block)
            for n, (buf, hbm) in enumerate(((oc if out else pc, first), (oo if out else po, second))):
                there = hbm.at[2 * lax.rem(j, 2) + h]
                here = buf.at[slot, :, part]
                pair = (here, there) if out else (there, here)
                yield pltpu.make_async_copy(*pair, sems.at[slot, 2 * n + h])

    @pl.when(live == 1)
    def _():
        fetch(0, 0)
        if add:
            for m in moves(prev[0], prev[2], 0, 0, False, prev_sem):
                m.start()
        ct[...] = c_ref[...].T
        st[...] = dy_ref[...].T

        def step(j, _):
            slot = lax.rem(j, 2)
            arrived(slot)
            if add:
                for m in moves(prev[0], prev[2], 0, slot, False, prev_sem):
                    m.wait()

            @pl.when(j + 1 < PAIRS)
            def _():
                fetch(j + 1, 1 - slot)

            if add:

                @pl.when(j == 0)
                def _():
                    for m in moves(prev[0], prev[2], 1, 1, False, prev_sem):
                        m.start()

                @pl.when((j >= 1) & (j + 1 < PAIRS))
                def _():
                    for m in moves(prev[1], prev[3], j + 1, 1 - slot, False, prev_sem):
                        m.start()

            @pl.when(j >= 2)
            def _():
                for m in moves(ck, ok, 0, slot, True, out_sem):
                    m.wait()

            gc = nn(ct[...], q_buf[slot])
            go = nn(st[...], r_buf[slot])
            if add:
                gc = gc + pc[slot].astype(F32)
                go = go + po[slot].astype(F32)
            oc[slot] = gc.astype(BF16)
            oo[slot] = go.astype(BF16)

            @pl.when(j < 2)
            def _():
                for m in moves(ck, ok, j, slot, True, out_sem):
                    m.start()

            @pl.when(j >= 2)
            def _():
                for m in moves(cs, os_, j, slot, True, out_sem):
                    m.start()

            return 0

        lax.fori_loop(0, PAIRS, step, 0)
        for slot in range(2):
            for m in moves(ck, ok, 0, slot, True, out_sem):
                m.wait()


def weight_grad(z, sc, c, dy, r, q, prev, add):
    sds = jax.ShapeDtypeStruct
    shape = sds((PAIRS, z.width, z.block), BF16)
    return pl.pallas_call(
        functools.partial(weight_grad_kernel, z, add),
        in_specs=[SCALARS, WHOLE, WHOLE, ANYWHERE, ANYWHERE] + [ANYWHERE] * 4,
        out_specs=[ANYWHERE] * 4,
        out_shape=[shape] * 4,
        scratch_shapes=[
            pltpu.VMEM((z.width, z.rows), BF16),
            pltpu.VMEM((z.width, z.rows), BF16),
            pltpu.VMEM((2, z.rows, z.pair), BF16),
            pltpu.VMEM((2, z.rows, z.pair), BF16),
            pltpu.VMEM((2, z.width, z.pair), BF16),
            pltpu.VMEM((2, z.width, z.pair), BF16),
            pltpu.VMEM((2, z.width, z.pair), BF16),
            pltpu.VMEM((2, z.width, z.pair), BF16),
            pltpu.SemaphoreType.DMA((2, 2)),
            pltpu.SemaphoreType.DMA((2, 4)),
            pltpu.SemaphoreType.DMA((2, 4)),
        ],
        input_output_aliases={5: 0, 6: 1, 7: 2, 8: 3},
        compiler_params=pltpu.CompilerParams(vmem_limit_bytes=VMEM_LIMIT),
        cost_estimate=pl.CostEstimate(flops=5_400_000_000, transcendentals=0, bytes_accessed=20_000_000),
    )(sc, c, dy, r, q, *prev)


class Moves:
    def __init__(self):
        self.sections, self.dp = lax.axis_size("section"), lax.axis_size("dp")

    def flip(self, array, sections, bit):
        pairs = [(s * self.dp + i, s * self.dp + (i ^ bit)) for s in sections for i in range(self.dp)]
        return lax.ppermute(array, ("section", "dp"), pairs)

    def shift(self, array, *routes):
        pairs = [(a * self.dp + i, b * self.dp + i) for a, b in routes for i in range(self.dp)]
        return lax.ppermute(array, ("section", "dp"), pairs)


CORE, ACROSS, ALONG = 1, 2, 4


def gather_way(move, own, sections, first, second):
    one = move.flip(own, sections, first)
    pair = jnp.stack([own, one])
    stack = move.flip(pair, sections, second)
    core_first = move.flip(pair, sections, CORE)
    core_stack = move.flip(stack, sections, CORE)
    return [own, one, stack, core_first, core_stack]


def gather(move, fast, own, sections):
    ci, co, pack = own
    if fast:
        token = gather_way(move, pack, sections, ACROSS, ALONG)
        pack_all = jnp.concatenate([token[0][None], token[1][None], token[2], token[3], token[4]])
        pack_all = pack_all.reshape(-1, pack.shape[1])
        return (
            gather_way(move, ci, sections, ACROSS, ALONG) + gather_way(move, co, sections, ALONG, ACROSS),
            pack_all,
        )
    ci_all = lax.all_gather(ci, "dp", axis=1, tiled=True)
    co_all = lax.all_gather(co, "dp", axis=0, tiled=True)
    pack_all = lax.all_gather(pack, "dp", axis=0, tiled=True)
    ci_block, co_block = ci_all.shape[1] // PIECES, co_all.shape[0] // PIECES
    number = [piece_number(r) for r in range(PIECES)]
    a = [ci_all[:, n * ci_block : (n + 1) * ci_block] for n in number]
    b = [co_all[n * co_block : (n + 1) * co_block] for n in number]
    first = [a[0], a[1], jnp.stack(a[2:4]), jnp.stack(a[4:6]), jnp.stack(a[6:8])]
    second = [b[0], b[2], jnp.stack([b[1], b[3]]), jnp.stack([b[4], b[6]]), jnp.stack([b[5], b[7]])]
    return first + second, pack_all


def add(a, b):
    return a.astype(F32) + b.astype(F32)


def scatter(move, fast, grads, pack, sections):
    ck, cs, ok, os_ = grads
    if not fast:
        number = [piece_number(r) for r in range(PIECES)]
        order = [number.index(b) for b in range(PIECES)]

        def whole(keep, send):
            pieces = [keep[r] if r < 4 else send[r - 4] for r in order]
            return lax.psum_scatter(
                jnp.concatenate(pieces, axis=1).astype(F32), "dp", scatter_dimension=1, tiled=True
            )

        token = lax.psum_scatter(pack.astype(F32), "dp", scatter_dimension=0, tiled=True)
        return whole(ck, cs), whole(ok, os_), token
    token = pack.reshape(2, 4, pack.shape[0] // PIECES, pack.shape[1])
    c = add(ck, move.flip(cs, sections, CORE)).astype(BF16)
    o = add(ok, move.flip(os_, sections, CORE)).astype(BF16)
    t = add(token[0], move.flip(token[1], sections, CORE)).astype(BF16)
    c_in = move.flip(c[2:4], sections, ALONG)
    o_in = move.flip(o[1::2], sections, ACROSS)
    t_in = move.flip(t[2:4], sections, ALONG)
    c = add(c[0:2], c_in).astype(BF16)
    o = add(o[0::2], o_in).astype(BF16)
    t = add(t[0:2], t_in).astype(BF16)
    return (
        add(c[0], move.flip(c[1], sections, ACROSS)),
        add(o[0], move.flip(o[1], sections, ALONG)),
        add(t[0], move.flip(t[1], sections, ACROSS)),
    )


def split_float(v):
    high = lax.reduce_precision(v, 8, 7)
    rest = v - high
    middle = lax.reduce_precision(rest, 8, 7)
    return [high, middle, rest - middle]


def pad_columns(v, width):
    return jnp.pad(v, ((0, 0), (0, width - v.shape[1])))


def shards(
    images,
    cotangent,
    groups,
    norm_gain,
    norm_bias,
    small_in,
    small_out,
    large_in,
    large_out,
    token_bias,
    small_patch_bias,
    large_patch_bias,
    channel_in,
    channel_out,
    channel_bias,
):
    move = Moves()
    section, dp = lax.axis_index("section"), lax.axis_index("dp")
    n_dp = lax.axis_size("dp")
    fast = n_dp == PIECES
    width, own_tokens = images.shape[3], small_in.shape[2]
    z = Sizes(images.shape[2], small_in.shape[1], width, own_tokens * n_dp, channel_in.shape[2] * n_dp)

    biases = lax.dynamic_slice_in_dim(token_bias[0], dp * own_tokens, own_tokens, axis=1)
    columns = split_float(biases[1]) + split_float(biases[0])
    bias_columns = jnp.stack(columns, axis=1).astype(BF16)
    pack = jnp.concatenate(
        [
            large_in[0].T,
            pad_columns(bias_columns, z.large_pad - z.rows),
            pad_columns(large_out[0], z.large_pad),
            pad_columns(small_in[0].T, z.small_pad),
            pad_columns(small_out[0], z.small_pad),
        ],
        axis=1,
    )
    hidden_bias = channel_bias[0, : z.hidden].reshape(PIECES, z.block)
    vectors = jnp.concatenate(
        [
            norm_gain[0],
            norm_bias[0],
            channel_bias[0, z.hidden :][None],
            pad_columns(large_patch_bias, width),
            pad_columns(jnp.concatenate([small_patch_bias, small_patch_bias], axis=1), width),
            jnp.zeros((1, width), F32),
            pad_columns(hidden_bias, width),
        ],
        axis=0,
    )
    own = (channel_in[0], channel_out[0], pack)

    to_a = [move.shift(w, (1, 2), (2, 1)) for w in own + (vectors,)]
    far = [move.shift(w, (3, 2)) for w in own + (vectors,)]
    last = [jnp.where(section == 2, w, move.shift(w, (2, 1))) for w in far]
    set_a, pack_a = gather(move, fast, own, (0, 1, 2))
    set_b, pack_b = gather(move, fast, to_a[:3], (1, 2))
    set_c, pack_c = gather(move, fast, last[:3], (1, 2))
    on_two = section == 2
    pack_1, pack_2 = jnp.where(on_two, pack_b, pack_a), jnp.where(on_two, pack_a, pack_b)
    vec_1, vec_2 = jnp.where(on_two, to_a[3], vectors), jnp.where(on_two, vectors, to_a[3])
    vec_3 = last[3]

    kind_0, kind_1 = groups[0, 0], groups[1, 0]
    here = dp if fast else 0

    def scalars(live, kind, select):
        at = lax.iota(jnp.int32, 4)
        live, select = live.astype(jnp.int32), jnp.asarray(select, jnp.int32)
        return jnp.where(at == 0, live, jnp.where(at == 1, kind, jnp.where(at == 2, here, select)))

    low = section == 0
    high = (section == 1) | on_two
    kind_b = jnp.where(on_two, kind_1, kind_0)

    def forward(sc, x, pack, v, sets):
        m, c, a, g, s = token_forward(z, sc, x, pack, v)
        out, r, slope = channel_forward(z, sc, c, m, v, sets)
        return out, (x, m, c, a, g, s, r, slope)

    sc_0, sc_1 = scalars(low, kind_0, 0), scalars(low, kind_1, 0)
    out_00, kept_00 = forward(sc_0, images[0, 0], pack_a, vectors, [set_a])
    hop_0 = move.shift(out_00, (0, 1))
    out_01, kept_01 = forward(sc_1, images[1, 0], pack_a, vectors, [set_a])
    hop_1 = move.shift(out_01, (0, 2))

    sc_b1, sc_b2 = scalars(high, kind_b, on_two), scalars(high, kind_b, section == 1)
    sc_b3 = scalars(high, kind_b, 0)
    x_1 = jnp.where(on_two, hop_1, hop_0)
    out_1, kept_1 = forward(sc_b1, x_1, pack_1, vec_1, [set_a, set_b])
    out_2, kept_2 = forward(sc_b2, out_1, pack_2, vec_2, [set_a, set_b])
    out_3, kept_3 = forward(sc_b3, out_2, pack_c, vec_3, [set_c])

    row = lax.broadcasted_iota(jnp.int32, (z.rows, 1), 0)
    used = (row < 2 * z.small) | (kind_b == 1)
    dy_3 = jnp.where(used, jnp.where(on_two, cotangent[1, 0], cotangent[0, 0]), 0)

    def channel_back(sc, dy, kept, v, sets):
        x, m, c, a, g, s, r, slope = kept
        return channel_backward(z, sc, dy, slope, m, v, sets)

    def token_back(sc, dm, kept, pack, v, prev, more):
        x, m, c, a, g, s, r, slope = kept
        return token_backward(z, sc, dm, x, a, pack, g, s, v, prev, more)

    def weights_back(sc, dy, dq, kept, prev, more):
        x, m, c, a, g, s, r, slope = kept
        return weight_grad(z, sc, c, dy, r, dq, prev, more)

    blank = [jnp.zeros((PAIRS, z.width, z.block), BF16) for _ in range(4)]
    blank_pack = jnp.zeros((z.tokens, z.pack), BF16)

    def backward(sc, dy, kept, pack, v, sets):
        dm, dq, dv_c, dh = channel_back(sc, dy, kept, v, sets)
        dx, dpack, dv_t, db = token_back(sc, dm, kept, pack, v, blank_pack, False)
        return dx, dpack, dq, (dv_c, dh, dv_t, db)

    dx_3, dpack_3, dq_3, small_3 = backward(sc_b3, dy_3, kept_3, pack_c, vec_3, [set_c])
    grads_3 = weights_back(sc_b3, dy_3, dq_3, kept_3, blank, False)
    dx_2, dpack_2, dq_2, small_2 = backward(sc_b2, dx_3, kept_2, pack_2, vec_2, [set_a, set_b])
    dx_1, dpack_1, dq_1, small_1 = backward(sc_b1, dx_2, kept_1, pack_1, vec_1, [set_a, set_b])
    back_0 = move.shift(dx_1, (1, 0))
    back_1 = move.shift(dx_1, (2, 0))
    grads_2 = weights_back(sc_b2, dx_3, dq_2, kept_2, blank, False)
    grads_1 = weights_back(sc_b1, dx_2, dq_1, kept_1, blank, False)

    dm, dq_00, dv_c0, dh_0 = channel_back(sc_0, back_0, kept_00, vectors, [set_a])
    grads_1 = weights_back(sc_0, back_0, dq_00, kept_00, grads_1, False)
    dx_00, dpack_1, dv_t0, db_0 = token_back(sc_0, dm, kept_00, pack_a, vectors, dpack_1, False)
    dm, dq_01, dv_c1, dh_1 = channel_back(sc_1, back_1, kept_01, vectors, [set_a])
    grads_1 = weights_back(sc_1, back_1, dq_01, kept_01, grads_1, True)
    dx_01, dpack_1, dv_t1, db_1 = token_back(sc_1, dm, kept_01, pack_a, vectors, dpack_1, True)

    share_3 = scatter(move, fast, grads_3, dpack_3, (1, 2))
    share_2 = scatter(move, fast, grads_2, dpack_2, (1, 2))
    share_1 = scatter(move, fast, grads_1, dpack_1, (0, 1, 2))

    def place(w_1, w_2, w_3, narrow):
        low_type = BF16 if narrow else F32
        in_1 = move.shift(w_1.astype(low_type), (2, 1)).astype(F32)
        in_2 = move.shift(w_2.astype(low_type), (1, 2)).astype(F32)
        both_3 = w_3 + move.shift(w_3.astype(low_type), (1, 2)).astype(F32)
        in_3 = move.shift(both_3.astype(low_type), (2, 3)).astype(F32)
        return jnp.where(
            section == 0, w_1, jnp.where(section == 1, w_1 + in_1, jnp.where(on_two, w_2 + in_2, in_3))
        )

    d_ci, d_co, d_pack = [place(a, b, c, True) for a, b, c in zip(share_1, share_2, share_3)]

    def in_order(db):
        if not fast:
            return db
        v = db.reshape(8, 2, 2, 2, own_tokens).transpose(0, 2, 3, 1, 4)
        for axis, bit in ((1, ALONG), (2, ACROSS), (3, CORE)):
            v = jnp.where((dp & bit) != 0, jnp.flip(v, axis), v)
        return v.reshape(8, z.tokens)

    def lines(dv_c, dh, dv_t, db):
        db = in_order(db)
        return jnp.concatenate(
            [
                dv_c + dv_t,
                pad_columns(dh, width),
                pad_columns(db, width),
            ]
        )

    zero_lines = lines(dv_c0, dh_0, dv_t0, db_0) + lines(dv_c1, dh_1, dv_t1, db_1)
    line_1 = jnp.where(low, zero_lines, lines(*small_1))
    summed = lax.psum((line_1, lines(*small_2), lines(*small_3)), "dp")
    total = place(*summed, False)

    d_gain, d_shift = total[0:2], total[2:4]
    d_bias = jnp.concatenate([total[8:16, : z.block].reshape(-1), total[4]])
    d_large_patch = total[5, : z.rows]
    d_small_patch = total[6, : z.small] + total[6, z.small : 2 * z.small]
    d_token = total[16:18, : z.tokens]

    def spread(f_0, f_1, w_1, w_2, w_3):
        crossed = move.shift(jnp.where(on_two, w_1, w_2), (1, 2), (2, 1))
        third_0, third_1 = move.shift(w_3, (1, 3)), move.shift(w_3, (2, 3))
        slot_0 = jnp.where(low, f_0, jnp.where(section == 1, w_1, jnp.where(on_two, crossed, third_0)))
        slot_1 = jnp.where(low, f_1, jnp.where(section == 1, crossed, jnp.where(on_two, w_2, third_1)))
        return jnp.stack([slot_0, slot_1])[None, :, None]

    outputs = spread(out_00, out_01, out_1, out_2, out_3)
    input_grads = spread(dx_00, dx_01, dx_1, dx_2, dx_3)
    return (
        outputs,
        input_grads,
        d_gain[None],
        d_shift[None],
        d_pack[:, z.c_s1 : z.c_s1 + z.small].T[None],
        d_pack[:, z.c_s2 : z.c_s2 + z.small][None],
        d_pack[:, z.c_l1 : z.c_l1 + z.rows].T[None],
        d_pack[:, z.c_l2 : z.c_l2 + z.rows][None],
        d_token[None],
        d_small_patch[None],
        d_large_patch[None],
        d_ci[None],
        d_co.T[None],
        d_bias[None],
    )


def solution(mesh):
    in_specs = (
        P(None, "dp", None, None),
        P(None, "dp", None, None),
        P(None, "dp"),
        P("section", None, None),
        P("section", None, None),
        P("section", None, "dp"),
        P("section", "dp", None),
        P("section", None, "dp"),
        P("section", "dp", None),
        P("section", None, None),
        P("section", None),
        P("section", None),
        P("section", None, "dp"),
        P("section", "dp", None),
        P("section", None),
    )
    out_specs = (
        P("section", None, "dp", None, None),
        P("section", None, "dp", None, None),
        P("section", None, None),
        P("section", None, None),
        P("section", None, "dp"),
        P("section", "dp", None),
        P("section", None, "dp"),
        P("section", "dp", None),
        P("section", None, None),
        P("section", None),
        P("section", None),
        P("section", None, "dp"),
        P("section", "dp", None),
        P("section", None),
    )
    return jax.shard_map(shards, mesh=mesh, in_specs=in_specs, out_specs=out_specs, check_vma=False)
```

```python
import types

import jax
import jax.numpy as jnp
from jax import lax
from jax.experimental import pallas as pl
from jax.experimental.pallas import tpu as pltpu
from jax.sharding import PartitionSpec as P

EPSILON = 1e-06
F32 = jnp.float32
BF16 = jnp.bfloat16
ROOT = 0.7978845608028654
CUBE = 0.044715
PIECES = 8
PAIRS = 4
CHUNK = 288
VMEM_LIMIT = 40 * 2**20
COST = pl.CostEstimate(flops=1, transcendentals=0, bytes_accessed=1)

IN_VMEM = pl.BlockSpec(memory_space=pltpu.VMEM)
SCALARS = pl.BlockSpec(memory_space=pltpu.SMEM)
HBM = pltpu.MemorySpace.HBM
ANYWHERE = pl.BlockSpec(memory_space=HBM)


def nn(a, b):
    return jnp.dot(a, b, preferred_element_type=F32)


def nt(a, b):
    return lax.dot_general(a, b, (((1,), (1,)), ((), ())), preferred_element_type=F32)


def tn(a, b):
    return lax.dot_general(a, b, (((0,), (0,)), ((), ())), preferred_element_type=F32)


def gelu_and_slope(v):
    square = v * v
    half = 0.5 * jnp.tanh(v * (ROOT + (ROOT * CUBE) * square)) + 0.5
    out = v * half
    return out, half + out * ((1.0 - half) * (2.0 * ROOT + (6.0 * ROOT * CUBE) * square))


def centre(v):
    c = v - jnp.mean(v, axis=-1, keepdims=True)
    r = lax.rsqrt(jnp.mean(c * c, axis=-1, keepdims=True) + EPSILON)
    return c * r, r


def norm_back(grad, xhat, rstd, gain):
    g = grad * gain
    m1 = jnp.mean(g, axis=-1, keepdims=True)
    m2 = jnp.mean(g * xhat, axis=-1, keepdims=True)
    return rstd * (g - m1 - xhat * m2)


def fold(v):
    return v.reshape(v.shape[0] // 8, 8, v.shape[1]).sum(axis=0)


def piece_number(r):
    return ((r >> 2) & 1) | ((r & 1) << 1) | (((r >> 1) & 1) << 2)


class Sizes:
    def __init__(self, rows, small, width, tokens, hidden):
        self.rows, self.small, self.width, self.tokens, self.hidden = rows, small, width, tokens, hidden
        self.large_pad = -(-rows // 128) * 128
        self.small_pad = -(-small // 128) * 128
        self.pack = 2 * (self.large_pad + self.small_pad)
        self.c_l1, self.c_l2 = 0, self.large_pad
        self.c_s1 = 2 * self.large_pad
        self.c_s2 = self.c_s1 + self.small_pad
        self.bias_col = rows
        self.block = hidden // PIECES
        self.pair = hidden // PAIRS
        self.own_tokens = tokens // PIECES
        self.chunks = -(-self.pack // self.block)
        self.half = self.chunks * self.own_tokens // 2


SDS = jax.ShapeDtypeStruct


def call(name, body, ins, outs, scratch, aliases=(), gates=()):
    ins = {**ins, **{f"gate{n}": (gate, ANYWHERE) for n, gate in enumerate(gates)}}
    names = [*ins, *outs, *scratch]

    def kernel(*refs):
        body(types.SimpleNamespace(**dict(zip(names, refs))))

    kernel.__name__ = name
    places = {list(ins).index(a): list(outs).index(b) for a, b in aliases}
    results = pl.pallas_call(
        kernel,
        name=name,
        in_specs=[spec for _, spec in ins.values()],
        out_specs=[spec for _, _, spec in outs.values()],
        out_shape=[HBM(shape, dtype) if spec is ANYWHERE else SDS(shape, dtype) for shape, dtype, spec in outs.values()],
        scratch_shapes=list(scratch.values()),
        input_output_aliases=places,
        compiler_params=pltpu.CompilerParams(vmem_limit_bytes=VMEM_LIMIT),
        cost_estimate=COST,
    )(*[pltpu.with_memory_space_constraint(a, HBM) if spec is ANYWHERE else a for a, spec in ins.values()])
    return dict(zip(outs, results))


class Copies:
    def __init__(self, sem):
        self.sem, self.count = sem, 0

    def start(self, source, target):
        copy = pltpu.make_async_copy(source, target, self.sem.at[self.count])
        self.count += 1
        copy.start()
        return copy


def in_piece_order(refs, second_way):
    own, one, stack, first, far = refs
    if second_way:
        return [own, stack.at[0], one, stack.at[1], first.at[0], far.at[0], first.at[1], far.at[1]]
    return [own, one, stack.at[0], stack.at[1], first.at[0], first.at[1], far.at[0], far.at[1]]


def pack_parts(z, first, first_row, second, second_row, pack):
    for i in range(z.chunks):
        lo, hi = i * z.block, min(z.pack, (i + 1) * z.block)
        start, end = i * z.own_tokens, (i + 1) * z.own_tokens
        cut = min(max(z.half, start), end)
        if cut > start:
            rows = pl.ds(first_row + start, cut - start)
            yield first.at[rows, 0 : hi - lo], pack.at[0 : cut - start, lo:hi]
        if end > cut:
            rows = pl.ds(second_row + cut - z.half, end - cut)
            yield second.at[rows, 0 : hi - lo], pack.at[cut - start : end - start, lo:hi]


class PlainSet:
    count = 15

    def __init__(self, z, refs):
        self.ci, self.co = in_piece_order(refs[0:5], False), in_piece_order(refs[5:10], True)
        self.packs = in_piece_order(refs[10:15], False)

    def first(self, z, r, target):
        return [(self.ci[r], target)]

    def second(self, z, r, target):
        return [(self.co[r], target)]

    def pack(self, z, r, target):
        return [(self.packs[r], target)]


class PackSet:
    count = 5

    def __init__(self, z, refs):
        self.packs = in_piece_order(refs, False)

    def pack(self, z, r, target):
        return [(self.packs[r], target)]


class ParcelSet:
    count = 10

    def __init__(self, z, refs):
        self.a, self.b = in_piece_order(refs[0:5], False), in_piece_order(refs[5:10], True)

    def first(self, z, r, target):
        return [(self.a[r].at[0 : z.width], target)]

    def second(self, z, r, target):
        for i in range(z.width // z.block):
            rows = pl.ds(z.half + i * z.block, z.block)
            yield self.b[r].at[rows], target.at[:, i * z.block : (i + 1) * z.block]

    def pack(self, z, r, target):
        return pack_parts(z, self.a[r], z.width, self.b[r], 0, target)


def open_sets(z, r, sets):
    opened = []
    for n, (kind, _) in enumerate(sets):
        opened.append(kind(z, [getattr(r, f"w{n}_{k}") for k in range(kind.count)]))
    return opened


def set_inputs(sets):
    return {f"w{n}_{k}": (a, ANYWHERE) for n, (_, arrays) in enumerate(sets) for k, a in enumerate(arrays)}


def for_chosen(sets, select, act):
    for n, one in enumerate(sets):
        if len(sets) == 1:
            act(one)
        else:
            pl.when(select == n)(lambda one=one: act(one))


def start_pack(z, r, sets, select):
    def act(one):
        for p in range(PIECES):
            rows = pl.ds(p * z.own_tokens, z.own_tokens)
            for source, target in one.pack(z, p, r.t_buf.at[rows]):
                pltpu.make_async_copy(source, target, r.t_sem).start()

    for_chosen(sets, select, act)


def wait_pack(r):
    pltpu.make_async_copy(r.t_buf, r.t_buf, r.t_sem).wait()


def start_pair(z, r, sets, select, j, slot):
    def act(one):
        for k in range(PAIRS):

            @pl.when(j == k)
            def _():
                for h in range(2):
                    part = pl.ds(h * z.block, z.block)
                    for source, target in one.first(z, 2 * k + h, r.ci_buf.at[slot, :, part]):
                        pltpu.make_async_copy(source, target, r.ci_sem.at[slot]).start()
                    for source, target in one.second(z, 2 * k + h, r.co_buf.at[slot, part, :]):
                        pltpu.make_async_copy(source, target, r.co_sem.at[slot]).start()

    for_chosen(sets, select, act)


def wait_pair(r, slot):
    pltpu.make_async_copy(r.ci_buf.at[slot], r.ci_buf.at[slot], r.ci_sem.at[slot]).wait()
    pltpu.make_async_copy(r.co_buf.at[slot], r.co_buf.at[slot], r.co_sem.at[slot]).wait()


def weight_scratch(z):
    return {
        "ci_buf": pltpu.VMEM((2, z.width, z.pair), BF16),
        "co_buf": pltpu.VMEM((2, z.pair, z.width), BF16),
        "ci_sem": pltpu.SemaphoreType.DMA((2,)),
        "co_sem": pltpu.SemaphoreType.DMA((2,)),
    }


def pack_scratch(z):
    return {"t_buf": pltpu.VMEM((z.tokens, z.pack), BF16), "t_sem": pltpu.SemaphoreType.DMA(())}


def pair_bias(z, v_ref, dp, j):
    rows = [8 + (dp ^ piece_number(2 * j + h)) for h in range(2)]
    return jnp.concatenate([v_ref[pl.ds(r, 1), 0 : z.block] for r in rows], axis=1)


def row_chunks(z, body, init=0):
    return lax.fori_loop(0, z.rows // CHUNK, lambda i, c: body(pl.ds(pl.multiple_of(i * CHUNK, CHUNK), CHUNK), c), init)


def token_forward_body(z, r, kind, copies):
    gain1, gain2, shift1, shift2 = r.v[0:1, :], r.v[1:2, :], r.v[2:3, :], r.v[3:4, :]

    def first(at, carry):
        xhat, _r = centre(r.x_buf[at, :].astype(F32))
        r.a_buf[at, :] = (xhat * gain1 + shift1).astype(BF16)
        return carry

    row_chunks(z, first)
    done = [copies.start(r.a_buf, r.a)]
    columns = r.v[0:8, :].T
    wait_pack(r)

    @pl.when(kind == 1)
    def _():
        w1 = r.t_buf[:, z.c_l1 : z.c_l1 + z.rows]
        b = [r.t_buf[:, z.bias_col + k : z.bias_col + k + 1].astype(F32) for k in range(3)]
        g, s = gelu_and_slope(nn(w1, r.a_buf[...]) + (b[0] + b[1] + b[2]))
        g = g.astype(BF16)
        r.g_buf[0 : z.tokens, :] = g
        r.s_buf[0 : z.tokens, :] = s.astype(BF16)
        w2 = r.t_buf[:, z.c_l2 : z.c_l2 + z.rows]
        r.m_buf[...] = r.x_buf[...].astype(F32) + (tn(w2, g) + columns[0 : z.rows, 5:6])

    @pl.when(kind == 0)
    def _():
        w1 = r.t_buf[:, z.c_s1 : z.c_s1 + z.small_pad]
        w2 = r.t_buf[:, z.c_s2 : z.c_s2 + z.small_pad]
        b = [r.t_buf[:, z.bias_col + 3 + k : z.bias_col + 4 + k].astype(F32) for k in range(3)]
        r.m_buf[...] = r.a_buf[...].astype(F32)
        normed = [r.m_buf[k * z.small : k * z.small + z.small_pad, :].astype(BF16) for k in range(2)]
        r.m_buf[...] = r.x_buf[...].astype(F32)
        for image in range(2):
            lo = image * z.small
            own = slice(image * z.tokens, (image + 1) * z.tokens)
            g, s = gelu_and_slope(nn(w1, normed[image]) + (b[0] + b[1] + b[2]))
            g = g.astype(BF16)
            r.g_buf[own, :] = g
            r.s_buf[own, :] = s.astype(BF16)
            mixed = tn(w2, g) + columns[0 : z.small_pad, 6:7]
            r.m_buf[lo : lo + z.small, :] = r.m_buf[lo : lo + z.small, :] + mixed[0 : z.small, :]

    done += [copies.start(r.g_buf, r.g), copies.start(r.s_buf, r.s), copies.start(r.m_buf, r.m)]

    def second(at, carry):
        m = r.m_buf[at, :]
        xhat, _r = centre(m)
        r.c_buf[at, :] = (xhat * gain2 + shift2).astype(BF16)
        r.acc[at, :] = m
        return carry

    row_chunks(z, second)
    return done + [copies.start(r.c_buf, r.c)]


def channel_forward_body(z, r, sets, kind, dp, select):
    parts = 2
    rows = z.rows // parts

    def out_copies(j, slot):
        return (
            pltpu.make_async_copy(r.r_buf.at[slot], r.r.at[j], r.out_sem.at[slot, 0]),
            pltpu.make_async_copy(r.q_buf.at[slot], r.slope.at[j], r.out_sem.at[slot, 1]),
        )

    def step(j, _):
        slot = lax.rem(j, 2)
        wait_pair(r, slot)

        @pl.when(j + 1 < PAIRS)
        def _():
            start_pair(z, r, sets, select, j + 1, 1 - slot)

        @pl.when(j >= 2)
        def _():
            for copy in out_copies(0, slot):
                copy.wait()

        bias = pair_bias(z, r.v, dp, j)
        for i in range(parts):
            at = pl.ds(i * rows, rows)
            g, s = gelu_and_slope(nn(r.c_buf[at, :], r.ci_buf[slot]) + bias)
            g = g.astype(BF16)
            r.r_buf[slot, at, :] = g
            r.q_buf[slot, at, :] = s.astype(BF16)
            r.acc[at, :] += nn(g, r.co_buf[slot])
        for copy in out_copies(j, slot):
            copy.start()
        return 0

    lax.fori_loop(0, PAIRS, step, 0)
    used = lax.broadcasted_iota(jnp.int32, (z.rows, 1), 0) < jnp.where(kind == 1, z.rows, 2 * z.small)
    r.out_buf[...] = jnp.where(used, r.acc[...] + r.v[4:5, :], 0.0).astype(BF16)
    for slot in range(2):
        for copy in out_copies(0, slot):
            copy.wait()


def forward(name, z, sc, v, sets, x=None, mid=None, token=True, channel=True, gates=()):
    wide, tall, hid = (z.rows, z.width), (2 * z.tokens, z.width), (PAIRS, z.rows, z.pair)
    ins = {"sc": (sc, SCALARS), "v": (v, IN_VMEM), **set_inputs(sets)}
    outs, scratch = {}, {"sem": pltpu.SemaphoreType.DMA((8,))}
    scratch["acc"] = pltpu.VMEM(wide, F32)
    scratch["c_buf"] = pltpu.VMEM(wide, BF16)
    if token:
        ins["x"] = (x, ANYWHERE)
        outs |= {"m": (wide, F32, ANYWHERE), "c": (wide, BF16, ANYWHERE), "a": (wide, BF16, ANYWHERE)}
        outs |= {"g": (tall, BF16, ANYWHERE), "s": (tall, BF16, ANYWHERE)}
        scratch |= {"x_buf": pltpu.VMEM(wide, BF16), "a_buf": pltpu.VMEM(wide, BF16), "m_buf": pltpu.VMEM(wide, F32)}
        scratch |= {"g_buf": pltpu.VMEM(tall, BF16), "s_buf": pltpu.VMEM(tall, BF16), **pack_scratch(z)}
    else:
        ins |= {"c": (mid[0], ANYWHERE), "m": (mid[1], ANYWHERE)}
    if channel:
        outs |= {"out": (wide, BF16, ANYWHERE), "r": (hid, BF16, ANYWHERE), "slope": (hid, BF16, ANYWHERE)}
        scratch |= {"r_buf": pltpu.VMEM((2, z.rows, z.pair), BF16), "q_buf": pltpu.VMEM((2, z.rows, z.pair), BF16)}
        scratch |= {"out_sem": pltpu.SemaphoreType.DMA((2, 2)), "out_buf": pltpu.VMEM(wide, BF16), **weight_scratch(z)}

    def body(r):
        live, kind, dp, select = r.sc[0], r.sc[1], r.sc[2], r.sc[3]

        @pl.when(live == 1)
        def _():
            opened = open_sets(z, r, sets)
            copies, done = Copies(r.sem), []
            if token:
                arrive = [copies.start(r.x, r.x_buf)]
                start_pack(z, r, opened, select)
            else:
                arrive = [copies.start(r.c, r.c_buf), copies.start(r.m, r.acc)]
            if channel:
                start_pair(z, r, opened, select, 0, 0)
            for copy in arrive:
                copy.wait()
            if token:
                done += token_forward_body(z, r, kind, copies)
            if channel:
                channel_forward_body(z, r, opened, kind, dp, select)
                done.append(copies.start(r.out_buf, r.out))
            for copy in done:
                copy.wait()

    return call(name, body, ins, outs, scratch, gates=gates)


def move_pack(z, keep, send, buf, sem, out):
    for p in range(PIECES):
        hbm, rows = (keep, send)[p // 4], pl.ds(p * z.own_tokens, z.own_tokens)
        for there, here in pack_parts(z, hbm.at[0, p % 4], z.width, hbm.at[1, p % 4], z.width, buf.at[rows]):
            pair = (here, there) if out else (there, here)
            pltpu.make_async_copy(*pair, sem).start()


def wait_all(buf, sem):
    pltpu.make_async_copy(buf, buf, sem).wait()


def token_backward_body(z, r, kind, add):
    ones = jnp.ones((8, z.width), BF16)
    by_patch = nt(ones, r.dvb[...])[0:1, :]
    wait_pack(r)

    def put(lo, value):
        hi = lo + value.shape[1]
        if add:
            value = value + r.t_out[:, lo:hi].astype(F32)
        r.t_out[:, lo:hi] = value.astype(BF16)

    if not add:
        r.t_out[...] = jnp.zeros_like(r.t_out)

    @pl.when(kind == 1)
    def _():
        r.dv[5:6, 0 : z.rows] = by_patch
        w1 = r.t_buf[:, z.c_l1 : z.c_l1 + z.rows]
        w2 = r.t_buf[:, z.c_l2 : z.c_l2 + z.rows]
        dz = (nn(w2, r.dvb[...]) * r.s_buf[0 : z.tokens, :].astype(F32)).astype(BF16)
        r.acc[...] = tn(w1, dz)
        put(z.c_l1, nt(dz, r.a_buf[...]))
        put(z.c_l2, nt(r.g_buf[0 : z.tokens, :], r.dvb[...]))
        r.db[1:2, :] = nt(ones, dz)[0:1, :]

    @pl.when(kind == 0)
    def _():
        r.dv[6:7, 0 : z.rows] = by_patch
        w1 = r.t_buf[:, z.c_s1 : z.c_s1 + z.small_pad]
        w2 = r.t_buf[:, z.c_s2 : z.c_s2 + z.small_pad]
        r.acc[...] = r.a_buf[...].astype(F32)
        normed = [r.acc[k * z.small : k * z.small + z.small_pad, :].astype(BF16) for k in range(2)]
        r.acc[...] = jnp.zeros_like(r.acc)
        dw1 = dw2 = dbias = 0.0
        for image in range(2):
            lo = image * z.small
            own = slice(image * z.tokens, (image + 1) * z.tokens)
            dv = r.dm_buf[lo : lo + z.small_pad, :].astype(BF16)
            dz = (nn(w2, dv) * r.s_buf[own, :].astype(F32)).astype(BF16)
            r.acc[lo : lo + z.small, :] = tn(w1, dz)[0 : z.small, :]
            dw1 = dw1 + nt(dz, normed[image])
            dw2 = dw2 + nt(r.g_buf[own, :], dv)
            dbias = dbias + nt(ones, dz)[0:1, :]
        put(z.c_s1, dw1)
        put(z.c_s2, dw2)
        r.db[0:1, :] = dbias

    gain1 = r.v[0:1, :]

    def back(at, carry):
        dgain, dshift = carry
        xhat, rstd = centre(r.x_buf[at, :].astype(F32))
        g = r.acc[at, :]
        r.x_buf[at, :] = (r.dm_buf[at, :] + norm_back(g, xhat, rstd, gain1)).astype(BF16)
        return (dgain + fold(g * xhat), dshift + fold(g))

    zero = jnp.zeros((8, z.width), F32)
    for row, total in zip((0, 2), row_chunks(z, back, (zero, zero))):
        r.dv[row : row + 1, :] = total.sum(axis=0, keepdims=True)


def channel_backward_body(z, r, sets, dp, select, weights, add):
    parts = 2
    rows = z.rows // parts

    def fetch(j, slot):
        found = [pltpu.make_async_copy(r.slope.at[j], r.slope_buf.at[slot], r.in_sem.at[slot, 0])]
        if weights:
            found.append(pltpu.make_async_copy(r.r.at[j], r.r_buf.at[slot], r.in_sem.at[slot, 1]))
        return found

    def start_fetch(j, slot):
        for copy in fetch(j, slot):
            copy.start()
        start_pair(z, r, sets, select, j, slot)

    def pieces(hbm, j, slot, out):
        for h in range(2):
            part = pl.ds(h * z.block, z.block)
            for n, buf in enumerate((r.oc, r.oo)):
                there, here = hbm.at[n, 2 * lax.rem(j, 2) + h, 0 : z.width], buf.at[slot, :, part]
                pair = (here, there) if out else (there, here)
                yield pltpu.make_async_copy(*pair, (r.out_sem if out else r.prev_sem).at[slot, 2 * n + h])

    start_fetch(0, 0)
    r.acc[...] = jnp.zeros_like(r.acc)
    if weights:
        r.ct[...] = r.c_buf[...].T
        r.st[...] = r.dy_buf[...].T

    def step(j, _):
        slot = lax.rem(j, 2)
        for copy in fetch(0, slot):
            copy.wait()
        wait_pair(r, slot)

        @pl.when(j + 1 < PAIRS)
        def _():
            start_fetch(j + 1, 1 - slot)

        @pl.when(j >= 2)
        def _():
            if weights:
                for copy in pieces(r.keep, 0, slot, True):
                    copy.wait()
            else:
                pltpu.make_async_copy(r.q_buf.at[slot], r.dq.at[0], r.out_sem.at[slot, 0]).wait()

        if weights and add:

            @pl.when(j < 2)
            def _():
                for copy in pieces(r.keep_in, j, slot, False):
                    copy.start()

            @pl.when(j >= 2)
            def _():
                for copy in pieces(r.send_in, j, slot, False):
                    copy.start()

        total = jnp.zeros((8, z.pair), F32)
        for i in range(parts):
            at = pl.ds(i * rows, rows)
            dq = nt(r.dy_buf[at, :], r.co_buf[slot]) * r.slope_buf[slot, at, :].astype(F32)
            total = total + fold(dq)
            dq = dq.astype(BF16)
            r.q_buf[slot, at, :] = dq
            r.acc[at, :] += nt(dq, r.ci_buf[slot])
        line = total.sum(axis=0, keepdims=True)
        for h in range(2):
            r.dh[pl.ds(dp ^ piece_number(2 * j + h), 1), :] = line[:, h * z.block : (h + 1) * z.block]
        if not weights:
            pltpu.make_async_copy(r.q_buf.at[slot], r.dq.at[j], r.out_sem.at[slot, 0]).start()
            return 0
        gc, go = nn(r.ct[...], r.q_buf[slot]), nn(r.st[...], r.r_buf[slot])
        if add:
            for copy in pieces(r.keep_in, 0, slot, False):
                copy.wait()
            gc, go = gc + r.oc[slot].astype(F32), go + r.oo[slot].astype(F32)
        r.oc[slot] = gc.astype(BF16)
        r.oo[slot] = go.astype(BF16)

        @pl.when(j < 2)
        def _():
            for copy in pieces(r.keep, j, slot, True):
                copy.start()

        @pl.when(j >= 2)
        def _():
            for copy in pieces(r.send, j, slot, True):
                copy.start()

        return 0

    lax.fori_loop(0, PAIRS, step, 0)
    gain2 = r.v[1:2, :]

    def back(at, carry):
        dgain, dshift, dout = carry
        xhat, rstd = centre(r.m_buf[at, :])
        dc = r.acc[at, :]
        dy = r.dy_buf[at, :].astype(F32)
        dm = dy + norm_back(dc, xhat, rstd, gain2)
        r.dm_buf[at, :] = dm
        r.dvb[at, :] = dm.astype(BF16)
        return (dgain + fold(dc * xhat), dshift + fold(dc), dout + fold(dy))

    zero = jnp.zeros((8, z.width), F32)
    for row, total in zip((1, 3, 4), row_chunks(z, back, (zero, zero, zero))):
        r.dv[row : row + 1, :] = total.sum(axis=0, keepdims=True)
    for slot in range(2):
        if weights:
            for copy in pieces(r.keep, 0, slot, True):
                copy.wait()
        else:
            pltpu.make_async_copy(r.q_buf.at[slot], r.dq.at[0], r.out_sem.at[slot, 0]).wait()


def backward(name, z, sc, v, sets, kept, dy, weights=True, prev=None, add=False, gates=()):
    wide, tall, hid = (z.rows, z.width), (2 * z.tokens, z.width), (PAIRS, z.rows, z.pair)
    grads = (2, PAIRS, z.width + z.half, z.block)
    ins = {"sc": (sc, SCALARS), "v": (v, IN_VMEM), **set_inputs(sets)}
    ins |= {"dy": (dy, ANYWHERE), "m": (kept["m"], ANYWHERE), "slope": (kept["slope"], ANYWHERE)}
    ins |= {k: (kept[k], ANYWHERE) for k in ("x", "a", "g", "s")}
    outs = {"dx": (wide, BF16, ANYWHERE), "dv": ((8, z.width), F32, IN_VMEM)}
    outs |= {"dh": ((8, z.block), F32, IN_VMEM), "db": ((8, z.tokens), F32, IN_VMEM)}
    two = pltpu.VMEM((2, z.rows, z.pair), BF16)
    scratch = {"sem": pltpu.SemaphoreType.DMA((12,)), "acc": pltpu.VMEM(wide, F32)}
    scratch |= {"dm_buf": pltpu.VMEM(wide, F32), "dvb": pltpu.VMEM(wide, BF16)}
    scratch |= {"dy_buf": pltpu.VMEM(wide, BF16), "m_buf": pltpu.VMEM(wide, F32), **weight_scratch(z)}
    scratch |= {"slope_buf": two, "q_buf": two}
    scratch |= {"in_sem": pltpu.SemaphoreType.DMA((2, 2)), "out_sem": pltpu.SemaphoreType.DMA((2, 4))}
    scratch |= {"x_buf": pltpu.VMEM(wide, BF16), "a_buf": pltpu.VMEM(wide, BF16), **pack_scratch(z)}
    scratch |= {"g_buf": pltpu.VMEM(tall, BF16), "s_buf": pltpu.VMEM(tall, BF16)}
    scratch |= {"t_out": pltpu.VMEM((z.tokens, z.pack), BF16), "t_out_sem": pltpu.SemaphoreType.DMA(())}
    aliases = []
    if weights:
        ins |= {"r": (kept["r"], ANYWHERE), "c": (kept["c"], ANYWHERE)}
        outs |= {"keep": (grads, BF16, ANYWHERE), "send": (grads, BF16, ANYWHERE)}
        turned, block = pltpu.VMEM((z.width, z.rows), BF16), pltpu.VMEM((2, z.width, z.pair), BF16)
        scratch |= {"r_buf": two, "c_buf": pltpu.VMEM(wide, BF16), "ct": turned, "st": turned, "oc": block, "oo": block}
        scratch["prev_sem"] = pltpu.SemaphoreType.DMA((2, 4))
        if prev is not None:
            ins |= {"keep_in": (prev[0], ANYWHERE), "send_in": (prev[1], ANYWHERE)}
            aliases += [("keep_in", "keep"), ("send_in", "send")]
    else:
        outs |= {"dq": (hid, BF16, ANYWHERE), "dpack": ((z.tokens, z.pack), BF16, ANYWHERE)}

    def body(r):
        live, kind, dp, select = r.sc[0], r.sc[1], r.sc[2], r.sc[3]

        @pl.when(live == 1)
        def _():
            opened = open_sets(z, r, sets)
            copies = Copies(r.sem)
            arrive = [copies.start(r.dy, r.dy_buf), copies.start(r.m, r.m_buf)]
            if weights:
                arrive.append(copies.start(r.c, r.c_buf))
            later = [copies.start(getattr(r, k), getattr(r, k + "_buf")) for k in ("x", "a", "g", "s")]
            start_pack(z, r, opened, select)
            if add:
                move_pack(z, r.keep_in, r.send_in, r.t_out, r.t_out_sem, False)
            for copy in arrive:
                copy.wait()
            r.dv[...] = jnp.zeros_like(r.dv)
            r.db[...] = jnp.zeros_like(r.db)
            channel_backward_body(z, r, opened, dp, select, weights, add)
            for copy in later:
                copy.wait()
            if add:
                wait_all(r.t_out, r.t_out_sem)
            token_backward_body(z, r, kind, add)
            done = copies.start(r.x_buf, r.dx)
            if weights:
                move_pack(z, r.keep, r.send, r.t_out, r.t_out_sem, True)
                wait_all(r.t_out, r.t_out_sem)
            else:
                copies.start(r.t_out, r.dpack).wait()
            done.wait()

    return call(name, body, ins, outs, scratch, aliases, gates)


def weight_grads(name, z, sc, dy, dq, dpack, kept, gates=()):
    wide = (z.rows, z.width)
    grads = (2, PAIRS, z.width + z.half, z.block)
    ins = {"sc": (sc, SCALARS), "dy": (dy, ANYWHERE), "dq": (dq, ANYWHERE), "r": (kept["r"], ANYWHERE), "c": (kept["c"], ANYWHERE)}
    ins["dpack"] = (dpack, ANYWHERE)
    outs = {"keep": (grads, BF16, ANYWHERE), "send": (grads, BF16, ANYWHERE)}
    two, block = pltpu.VMEM((2, z.rows, z.pair), BF16), pltpu.VMEM((2, z.width, z.pair), BF16)
    turned = pltpu.VMEM((z.width, z.rows), BF16)
    scratch = {"t_out": pltpu.VMEM((z.tokens, z.pack), BF16), "t_out_sem": pltpu.SemaphoreType.DMA(())}
    scratch |= {"sem": pltpu.SemaphoreType.DMA((3,)), "dy_buf": pltpu.VMEM(wide, BF16), "c_buf": pltpu.VMEM(wide, BF16)}
    scratch |= {"ct": turned, "st": turned, "r_buf": two, "q_buf": two, "oc": block, "oo": block}
    scratch |= {"in_sem": pltpu.SemaphoreType.DMA((2, 2)), "out_sem": pltpu.SemaphoreType.DMA((2, 4))}

    def body(r):
        def fetch(j, slot):
            return (
                pltpu.make_async_copy(r.r.at[j], r.r_buf.at[slot], r.in_sem.at[slot, 0]),
                pltpu.make_async_copy(r.dq.at[j], r.q_buf.at[slot], r.in_sem.at[slot, 1]),
            )

        def pieces(hbm, j, slot):
            for h in range(2):
                part = pl.ds(h * z.block, z.block)
                for n, buf in enumerate((r.oc, r.oo)):
                    there, here = hbm.at[n, 2 * lax.rem(j, 2) + h, 0 : z.width], buf.at[slot, :, part]
                    yield pltpu.make_async_copy(here, there, r.out_sem.at[slot, 2 * n + h])

        @pl.when(r.sc[0] == 1)
        def _():
            copies = Copies(r.sem)
            arrive = [copies.start(r.c, r.c_buf), copies.start(r.dy, r.dy_buf), copies.start(r.dpack, r.t_out)]
            for copy in fetch(0, 0):
                copy.start()
            for copy in arrive:
                copy.wait()
            move_pack(z, r.keep, r.send, r.t_out, r.t_out_sem, True)
            r.ct[...] = r.c_buf[...].T
            r.st[...] = r.dy_buf[...].T

            def step(j, _):
                slot = lax.rem(j, 2)
                for copy in fetch(0, slot):
                    copy.wait()

                @pl.when(j + 1 < PAIRS)
                def _():
                    for copy in fetch(j + 1, 1 - slot):
                        copy.start()

                @pl.when(j >= 2)
                def _():
                    for copy in pieces(r.keep, 0, slot):
                        copy.wait()

                r.oc[slot] = nn(r.ct[...], r.q_buf[slot]).astype(BF16)
                r.oo[slot] = nn(r.st[...], r.r_buf[slot]).astype(BF16)

                @pl.when(j < 2)
                def _():
                    for copy in pieces(r.keep, j, slot):
                        copy.start()

                @pl.when(j >= 2)
                def _():
                    for copy in pieces(r.send, j, slot):
                        copy.start()

                return 0

            lax.fori_loop(0, PAIRS, step, 0)
            for slot in range(2):
                for copy in pieces(r.keep, 0, slot):
                    copy.wait()
            wait_all(r.t_out, r.t_out_sem)

    return call(name, body, ins, outs, scratch, gates=gates)


class Moves:
    def __init__(self):
        self.sections, self.dp = lax.axis_size("section"), lax.axis_size("dp")

    def flip(self, array, sections, bit):
        pairs = [(s * self.dp + i, s * self.dp + (i ^ bit)) for s in sections for i in range(self.dp)]
        return lax.ppermute(array, ("section", "dp"), pairs)

    def shift(self, array, *routes):
        pairs = [(a * self.dp + i, b * self.dp + i) for a, b in routes for i in range(self.dp)]
        return lax.ppermute(array, ("section", "dp"), pairs)


CORE, ACROSS, ALONG = 1, 2, 4


def together(*values):
    return lax.optimization_barrier(values)


def gather(move, ci, co, pack):
    ci_all = lax.all_gather(ci, "dp", axis=1, tiled=True)
    co_all = lax.all_gather(co, "dp", axis=0, tiled=True)
    pack_all = lax.all_gather(pack, "dp", axis=0, tiled=True)
    ci_block, co_block, rows = ci_all.shape[1] // PIECES, co_all.shape[0] // PIECES, pack_all.shape[0] // PIECES
    number = [piece_number(r) for r in range(PIECES)]
    a = [ci_all[:, n * ci_block : (n + 1) * ci_block] for n in number]
    b = [co_all[n * co_block : (n + 1) * co_block] for n in number]
    c = [pack_all[n * rows : (n + 1) * rows] for n in range(PIECES)]
    first = [a[0], a[1], jnp.stack(a[2:4]), jnp.stack(a[4:6]), jnp.stack(a[6:8])]
    second = [b[0], b[2], jnp.stack([b[1], b[3]]), jnp.stack([b[4], b[6]]), jnp.stack([b[5], b[7]])]
    third = [c[0], c[1], jnp.stack(c[2:4]), jnp.stack(c[4:6]), jnp.stack(c[6:8])]
    return first + second + third


class Parcel:
    def __init__(self, fast, z, ci, co, pack, vectors):
        self.fast, self.z, self.vectors = fast, z, vectors
        if not fast:
            self.arrays = [ci, co, pack, vectors]
            return
        lanes = z.block
        wide = pad_columns(pack, z.chunks * lanes)
        thirds = jnp.stack(split_float(vectors)).astype(BF16).reshape(-1, vectors.shape[1])
        self.arrays = [jnp.concatenate([ci, self.rows(wide, lanes), self.rows(co, lanes), self.rows(thirds, lanes)])]

    @staticmethod
    def rows(v, lanes):
        return jnp.concatenate([v[:, i : i + lanes] for i in range(0, v.shape[1], lanes)])

    def open(self, arrays):
        if not self.fast:
            return arrays[:3], arrays[3]
        part = self.z.width + self.z.half
        rows = arrays[0][2 * part :]
        height = 3 * self.vectors.shape[0]
        thirds = jnp.concatenate([rows[i : i + height] for i in range(0, rows.shape[0], height)], axis=1)
        thirds = thirds.astype(F32).reshape(3, *self.vectors.shape)
        return (arrays[0][:part], arrays[0][part : 2 * part]), (thirds[0] + thirds[1]) + thirds[2]

    def first_gather(self, move, shares, sections):
        if not self.fast:
            return shares
        return [move.flip(share, sections, way) for share, way in zip(shares, (ACROSS, ALONG))]

    def second_gather(self, move, shares, ones, sections):
        if not self.fast:
            return ones, ones
        pairs = [jnp.stack(p) for p in zip(shares, ones)]
        return pairs, [move.flip(pair, sections, way) for pair, way in zip(pairs, (ALONG, ACROSS))]

    def core_gather(self, move, shares, ones, pairs, stacks, sections):
        if not self.fast:
            return PlainSet, gather(move, *shares)
        near = [move.flip(pair, sections, CORE) for pair in pairs]
        *near, a, b = together(*near, *stacks)
        far = [move.flip(stack, sections, CORE) for stack in (a, b)]
        arrays = []
        for parts in zip(shares, ones, (a, b), near, far):
            arrays += parts
        return ParcelSet, arrays


class Stage:
    def __init__(self):
        self.values = {}

    def end(self, **new):
        self.values.update(new)
        leaves, tree = jax.tree.flatten(self.values)
        self.values = jax.tree.unflatten(tree, lax.optimization_barrier(leaves))

    def __getitem__(self, name):
        return self.values[name]

    def take(self, name):
        return self.values.pop(name)


def three(*terms):
    return sum(t.astype(F32) for t in terms)


class GradSums:
    def __init__(self, move, fast, z, sections, *grads):
        self.move, self.fast, self.z, self.sections = move, fast, z, sections
        self.keep, self.send = [g["keep"] for g in grads], [g["send"] for g in grads]
        self.core_in = []

    def held(self):
        names = ("keep", "send", "core_in", "plane_in", "last_in") if not self.fast else ("keep", "core_in", "plane_in", "last_in")
        return {k: v for k, v in vars(self).items() if k in names}

    def hold(self, arrays):
        vars(self).update(arrays)

    def part(self, *at):
        return [a[at] for a in self.keep + self.core_in]

    def core(self, grads=None):
        if grads is not None:
            self.keep, self.send = self.keep + [grads["keep"]], self.send + [grads["send"]]
        if self.fast:
            self.core_in = self.core_in + [self.move.flip(a, self.sections, CORE) for a in self.send[len(self.core_in) :]]

    def plane_terms(self):
        return three(*self.part(0, slice(2, 4))).astype(BF16), three(*self.part(1, slice(1, 4, 2))).astype(BF16)

    def last_terms(self):
        c, o = self.plane_in
        return three(*self.part(0, 1), c[1]).astype(BF16), three(*self.part(1, 2), o[1]).astype(BF16)

    def plane(self, *others):
        self.step("plane", others, (ALONG, ACROSS))

    def last(self, *others):
        self.step("last", others, (ACROSS, ALONG))

    def step(self, name, others, ways):
        if not self.fast:
            return
        sums = (self,) + others
        terms = [getattr(s, name + "_terms")() for s in sums]
        for n, way in enumerate(ways):
            found = self.move.flip(jnp.stack([t[n] for t in terms]), self.sections, way)
            for k, one in enumerate(sums):
                vars(one).setdefault(name + "_new", []).append(found[k])
        for one in sums:
            setattr(one, name + "_in", vars(one).pop(name + "_new"))

    def share(self):
        z = self.z
        if self.fast:
            (c, o), (c_in, o_in) = self.plane_in, self.last_in
            return (jnp.stack([three(*self.part(0, 0), c[0], c_in), three(*self.part(1, 0), o[0], o_in)]),)
        number = [piece_number(r) for r in range(PIECES)]
        order = [number.index(b) for b in range(PIECES)]
        keep, send = three(*self.keep), three(*self.send)
        pieces = [jnp.concatenate([keep[n], send[n]]) for n in range(2)]

        def whole(found):
            found = jnp.concatenate([found[r, : z.width] for r in order], axis=1)
            return lax.psum_scatter(found, "dp", scatter_dimension=1, tiled=True)

        packs = [open_pack(z, pieces[0][r, z.width :], pieces[1][r, z.width :]) for r in range(PIECES)]
        token = lax.psum_scatter(jnp.concatenate(packs), "dp", scatter_dimension=0, tiled=True)
        return whole(pieces[0]), whole(pieces[1]), token


def open_pack(z, first, second):
    rows = jnp.concatenate([first, second])
    return jnp.concatenate([rows[i * z.own_tokens : (i + 1) * z.own_tokens] for i in range(z.chunks)], axis=1)[:, : z.pack]


def split_float(v):
    high = lax.reduce_precision(v, 8, 7)
    rest = v - high
    middle = lax.reduce_precision(rest, 8, 7)
    return [high, middle, rest - middle]


def pad_columns(v, width):
    return jnp.pad(v, ((0, 0), (0, width - v.shape[1])))


def shards(
    images,
    cotangent,
    groups,
    norm_gain,
    norm_bias,
    small_in,
    small_out,
    large_in,
    large_out,
    token_bias,
    small_patch_bias,
    large_patch_bias,
    channel_in,
    channel_out,
    channel_bias,
):
    move = Moves()
    section, dp = lax.axis_index("section"), lax.axis_index("dp")
    n_dp = lax.axis_size("dp")
    fast = n_dp == PIECES
    width, own_tokens = images.shape[3], small_in.shape[2]
    z = Sizes(images.shape[2], small_in.shape[1], width, own_tokens * n_dp, channel_in.shape[2] * n_dp)

    biases = lax.dynamic_slice_in_dim(token_bias[0], dp * own_tokens, own_tokens, axis=1)
    columns = split_float(biases[1]) + split_float(biases[0])
    bias_columns = jnp.stack(columns, axis=1).astype(BF16)
    pack = jnp.concatenate(
        [
            large_in[0].T,
            pad_columns(bias_columns, z.large_pad - z.rows),
            pad_columns(large_out[0], z.large_pad),
            pad_columns(small_in[0].T, z.small_pad),
            pad_columns(small_out[0], z.small_pad),
        ],
        axis=1,
    )
    hidden_bias = channel_bias[0, : z.hidden].reshape(PIECES, z.block)
    vectors = jnp.concatenate(
        [
            norm_gain[0],
            norm_bias[0],
            channel_bias[0, z.hidden :][None],
            pad_columns(large_patch_bias, width),
            pad_columns(jnp.concatenate([small_patch_bias, small_patch_bias], axis=1), width),
            jnp.zeros((1, width), F32),
            pad_columns(hidden_bias, width),
        ],
        axis=0,
    )
    own = (channel_in[0], channel_out[0], pack)

    planes_b, planes_all = (1, 2), (0, 1, 2)
    parcel_of = own
    if fast:
        ci_one = move.flip(own[0], planes_all, ACROSS)
        co_one = move.flip(own[1], planes_all, ALONG)
        pack_one = move.flip(own[2], planes_all, ACROSS)
        ci, co, ci_one, co_one, pack_one = together(own[0], own[1], ci_one, co_one, pack_one)
        ci_pair, co_pair, pack_pair = jnp.stack([own[0], ci_one]), jnp.stack([own[1], co_one]), jnp.stack([own[2], pack_one])
        pack_stack = move.flip(pack_pair, planes_all, ALONG)
        ci_stack = move.flip(ci_pair, planes_all, ALONG)
        co_stack = move.flip(co_pair, planes_all, ACROSS)
        pack_first = move.flip(pack_pair, planes_all, CORE)
        ci_first = move.flip(ci_pair, planes_all, CORE)
        co_first = move.flip(co_pair, planes_all, CORE)
        parcel_of = (ci, co, own[2])
        pack_far = move.flip(pack_stack, planes_all, CORE)
        packs_a = [own[2], pack_one, pack_stack, pack_first, pack_far]
    else:
        set_a = gather(move, *own)
        packs_a = set_a[10:]
    parcel = Parcel(fast, z, *parcel_of, vectors)
    near = [move.shift(w, (1, 2), (2, 1)) for w in parcel.arrays]
    far_2 = [move.shift(w, (3, 2)) for w in parcel.arrays]
    far_1 = [move.shift(w, (3, 1)) for w in parcel.arrays]
    packs_a = [(PackSet, packs_a)]
    on_two = section == 2

    kind_0, kind_1 = groups[0, 0], groups[1, 0]
    here = dp if fast else 0

    def scalars(live, kind, select):
        at = lax.iota(jnp.int32, 4)
        live, select = live.astype(jnp.int32), jnp.asarray(select, jnp.int32)
        return jnp.where(at == 0, live, jnp.where(at == 1, kind, jnp.where(at == 2, here, select)))

    low = section == 0
    high = (section == 1) | on_two
    kind_b = jnp.where(on_two, kind_1, kind_0)

    def in_order(db):
        if not fast:
            return db
        v = db.reshape(8, 2, 2, 2, own_tokens).transpose(0, 2, 3, 1, 4)
        for axis, bit in ((1, ALONG), (2, ACROSS), (3, CORE)):
            v = jnp.where((dp & bit) != 0, jnp.flip(v, axis), v)
        return v.reshape(8, z.tokens)

    def lines_of(b):
        return jnp.concatenate([b["dv"], pad_columns(b["dh"], width), pad_columns(in_order(b["db"]), width)])

    sc_0, sc_1 = scalars(low, kind_0, 0), scalars(low, kind_1, 0)
    kept_00 = forward("ft_0", z, sc_0, vectors, packs_a, x=images[0, 0], channel=False)
    kept_01 = forward("ft_1", z, sc_1, vectors, packs_a, x=images[1, 0], channel=False)
    kept_00["x"], kept_01["x"] = images[0, 0], images[1, 0]
    if fast:
        kept_00["c"], kept_01["c"], ci_stack, co_stack = together(kept_00["c"], kept_01["c"], ci_stack, co_stack)
        ci_far, co_far = move.flip(ci_stack, planes_all, CORE), move.flip(co_stack, planes_all, CORE)
        set_a = [own[0], ci_one, ci_stack, ci_first, ci_far, own[1], co_one, co_stack, co_first, co_far] + packs_a[0][1]
    weights_a = [(PlainSet, set_a)]
    kept_00 |= forward("fc_0", z, sc_0, vectors, weights_a, mid=(kept_00["c"], kept_00["m"]), token=False)
    hop_0 = move.shift(kept_00["out"], (0, 1))
    mid = (kept_01["c"], kept_01["m"])
    kept_01 |= forward("fc_1", z, sc_1, vectors, weights_a, mid=mid, token=False, gates=(kept_00["out"],))
    hop_1 = move.shift(kept_01["out"], (0, 2))

    *near, kept_01["slope"] = together(*near, kept_01["slope"])
    shares_b, other_vec = parcel.open(near)
    ones_b = parcel.first_gather(move, shares_b, planes_b)
    pairs_b, stacks_b = parcel.second_gather(move, shares_b, ones_b, planes_b)
    stacks_b[0], *far = together(stacks_b[0], *far_2, *far_1)
    weights_b = parcel.core_gather(move, shares_b, ones_b, pairs_b, stacks_b, planes_b)
    weights_ab = [weights_a[0], weights_b]
    vec_1, vec_2 = jnp.where(on_two, other_vec, vectors), jnp.where(on_two, vectors, other_vec)

    sc_b1, sc_b2 = scalars(high, kind_b, on_two), scalars(high, kind_b, section == 1)
    sc_b3 = scalars(high, kind_b, 0)
    far = [jnp.where(on_two, v, w) for v, w in zip(far[: len(far_2)], far[len(far_2) :])]
    shares_c, vec_3 = parcel.open(far)
    ones_c = parcel.first_gather(move, shares_c, planes_b)
    x_1 = jnp.where(on_two, hop_1, hop_0)
    kept_1 = forward("f_1", z, sc_b1, vec_1, weights_ab, x=x_1)
    out_1, *ones_c = together(kept_1["out"], *ones_c)
    pairs_c, stacks_c = parcel.second_gather(move, shares_c, ones_c, planes_b)
    kept_2 = forward("f_2", z, sc_b2, vec_2, weights_ab, x=out_1)
    out_2, *stacks_c = together(kept_2["out"], *stacks_c)
    weights_c = [parcel.core_gather(move, shares_c, ones_c, pairs_c, stacks_c, planes_b)]
    kept_1["x"], kept_2["x"] = x_1, out_1
    st = Stage()
    st.end(kept_00=kept_00, kept_01=kept_01, kept_1=kept_1, kept_2=kept_2, set_a=weights_a[0][1], set_b=weights_b[1], set_c=weights_c[0][1])
    kinds = [weights_b[0], weights_c[0][0]]
    vec = (vec_1, vec_2, vec_3)

    def sets():
        return [(PlainSet, st["set_a"]), (kinds[0], st["set_b"])]

    def crossed(w_1, w_2):
        return move.shift(jnp.where(on_two, w_1, w_2), (1, 2), (2, 1))

    kept_3 = forward("f_3", z, sc_b3, vec_3, [(kinds[1], st["set_c"])], x=st["kept_2"]["out"])
    kept_3["x"] = st["kept_2"]["out"]
    cross_out = crossed(st["kept_1"]["out"], st["kept_2"]["out"])
    row = lax.broadcasted_iota(jnp.int32, (z.rows, 1), 0)
    used = (row < 2 * z.small) | (kind_b == 1)
    dy_3 = jnp.where(used, jnp.where(on_two, cotangent[1, 0], cotangent[0, 0]), 0)
    st.end(kept_3=kept_3, cross_out=cross_out, dy_3=dy_3)

    b_3 = backward("b_3", z, sc_b3, vec_3, [(kinds[1], st.take("set_c"))], st["kept_3"], st.take("dy_3"))
    third_1 = [move.shift(st["kept_3"]["out"], (1, 3))]
    line_3 = lines_of(b_3)
    grads_3, dx_3 = {k: b_3[k] for k in ("keep", "send")}, b_3["dx"]
    st.end(grads_3=grads_3, dx_3=dx_3, line_3=line_3, third_1=third_1)
    sum_3 = GradSums(move, fast, z, planes_b, st.take("grads_3"))
    b_2 = backward("b_2", z, sc_b2, vec_2, sets(), st.take("kept_2"), st["dx_3"])
    sum_3.core()
    third_2 = [move.shift(st["kept_3"]["out"], (2, 3))]
    line_2 = lines_of(b_2)
    grads_2, dx_2 = {k: b_2[k] for k in ("keep", "send")}, b_2["dx"]
    st.end(grads_2=grads_2, dx_2=dx_2, line_2=line_2, sum_3=sum_3.held(), third_2=third_2, out_2=kept_2["out"])
    sum_3.hold(st.take("sum_3"))
    b_1 = backward("b_1", z, sc_b1, vec_1, sets(), st["kept_1"], st["dx_2"], weights=False)
    sum_3.plane()
    sum_2 = GradSums(move, fast, z, planes_b, st.take("grads_2"))
    sum_2.core()
    lines = jnp.stack([lines_of(b_1), st.take("line_2"), st.take("line_3")])
    b_1 = {k: b_1[k] for k in ("dx", "dq", "dpack")}
    st.end(b_1=b_1, lines=lines, sum_3=sum_3.held(), sum_2=sum_2.held())
    sum_3.hold(st.take("sum_3")), sum_2.hold(st.take("sum_2"))
    b_1 = st["b_1"]
    hop_0 = move.shift(b_1["dx"], (1, 0))
    w_1 = weight_grads("w_1", z, sc_b1, st["dx_2"], b_1["dq"], b_1["dpack"], st["kept_1"])
    sum_3.last()
    third_1 = st.take("third_1") + [move.shift(st["dx_3"], (1, 3))]
    held = {"sum_3": sum_3.held(), "sum_2": sum_2.held()}
    st.end(hop_0=hop_0, w_1=w_1, dx_1=b_1["dx"], third_1=third_1, **held)
    sum_3.hold(st.take("sum_3")), sum_2.hold(st.take("sum_2"))
    sum_2.plane()
    hop_1 = move.shift(st["dx_1"], (2, 0))
    share_3 = sum_3.share()

    weights_a = [(PlainSet, st["set_a"])]
    prev, gates = (st["w_1"]["keep"], st["w_1"]["send"]), ()
    back_00 = backward("b_00", z, sc_0, vectors, weights_a, st["kept_00"], st["hop_0"], prev=prev)
    prev, gates = (back_00["keep"], back_00["send"]), (back_00["dx"],)
    if fast:
        in_3 = move.shift(share_3[0].astype(BF16), (1, 2))
        gates += (*sum_2.plane_in, in_3)
    back_01 = backward("b_01", z, sc_1, vectors, weights_a, st["kept_01"], hop_1, prev=prev, add=True, gates=gates)
    dx_00, dx_01 = back_00["dx"], back_01["dx"]
    sum_1 = GradSums(move, fast, z, planes_all, back_01)
    sum_1.core()
    line_1 = jnp.where(low, lines_of(back_00) + lines_of(back_01), st["lines"][0])
    lines = jnp.concatenate([line_1[None], st["lines"][1:]])
    if fast:
        in_3 = move.shift((share_3[0] + in_3.astype(F32)).astype(BF16), (2, 3))
    sum_2.last()
    share_2 = sum_2.share()
    sum_1.plane()
    if fast:
        in_2 = move.shift(share_2[0].astype(BF16), (1, 2))
        lines = lines + move.flip(lines, planes_all, CORE)
        lines, in_3, *sum_1.plane_in = together(lines, in_3, *sum_1.plane_in)
        lines = lines + sum(move.flip(lines, planes_all, way) for way in (ACROSS, ALONG, ACROSS | ALONG))
    else:
        lines = lax.psum(lines, "dp")
    sum_1.last()
    if fast:
        in_2, *sum_1.last_in = together(in_2, *sum_1.last_in)
    share_1 = sum_1.share()
    if fast:
        in_1 = move.shift(share_1[0].astype(BF16), (2, 1))
    both = move.shift(jnp.where(on_two, jnp.stack([lines[0], lines[0]]), lines[1:]), (1, 2), (2, 1))
    line_3 = move.shift(lines[2] + both[1], (2, 3))
    third_2 = st["third_2"] + [move.shift(st["dx_3"], (2, 3))]
    cross_dx = crossed(st["dx_1"], st["dx_2"])

    def choose(w_0, w_1, w_2, w_3):
        return jnp.where(low, w_0, jnp.where(section == 1, w_1, jnp.where(on_two, w_2, w_3)))

    total = choose(lines[0], lines[0] + both[0], lines[1] + both[0], line_3)
    if fast:
        found = choose(share_1[0], share_1[0] + in_1, share_2[0] + in_2, in_3.astype(F32))
        d_ci, d_co = found[0, : z.width], found[1, : z.width]
        d_pack = open_pack(z, found[0, z.width :], found[1, z.width :])
    else:

        def place(w_1, w_2, w_3):
            low_1, low_2, low_3 = [w.astype(BF16) for w in (w_1, w_2, w_3)]
            both_3 = w_3 + move.shift(low_3, (1, 2))
            in_3 = move.shift(both_3.astype(BF16), (2, 3)).astype(F32)
            return choose(w_1, w_1 + move.shift(low_1, (2, 1)), w_2 + move.shift(low_2, (1, 2)), in_3)

        d_ci, d_co, d_pack = [place(*parts) for parts in zip(share_1, share_2, share_3)]

    d_gain, d_shift = total[0:2], total[2:4]
    d_bias = jnp.concatenate([total[8:16, : z.block].reshape(-1), total[4]])
    d_large_patch = total[5, : z.rows]
    d_small_patch = total[6, : z.small] + total[6, z.small : 2 * z.small]
    d_token = total[16:18, : z.tokens]

    def spread(f_0, f_1, w_1, w_2, other, third):
        slot_0 = jnp.where(low, f_0, jnp.where(section == 1, w_1, jnp.where(on_two, other, third[0])))
        slot_1 = jnp.where(low, f_1, jnp.where(section == 1, other, jnp.where(on_two, w_2, third[1])))
        return jnp.stack([slot_0, slot_1])[None, :, None]

    third = list(zip(st["third_1"], third_2))
    out_0, out_1 = st["kept_00"]["out"], st["kept_01"]["out"]
    outputs = spread(out_0, out_1, st["kept_1"]["out"], st["out_2"], st["cross_out"], third[0])
    input_grads = spread(dx_00, dx_01, st["dx_1"], st["dx_2"], cross_dx, third[1])
    return (
        outputs,
        input_grads,
        d_gain[None],
        d_shift[None],
        d_pack[:, z.c_s1 : z.c_s1 + z.small].T[None],
        d_pack[:, z.c_s2 : z.c_s2 + z.small][None],
        d_pack[:, z.c_l1 : z.c_l1 + z.rows].T[None],
        d_pack[:, z.c_l2 : z.c_l2 + z.rows][None],
        d_token[None],
        d_small_patch[None],
        d_large_patch[None],
        d_ci[None],
        d_co.T[None],
        d_bias[None],
    )


def solution(mesh):
    in_specs = (
        P(None, "dp", None, None),
        P(None, "dp", None, None),
        P(None, "dp"),
        P("section", None, None),
        P("section", None, None),
        P("section", None, "dp"),
        P("section", "dp", None),
        P("section", None, "dp"),
        P("section", "dp", None),
        P("section", None, None),
        P("section", None),
        P("section", None),
        P("section", None, "dp"),
        P("section", "dp", None),
        P("section", None),
    )
    out_specs = (
        P("section", None, "dp", None, None),
        P("section", None, "dp", None, None),
        P("section", None, None),
        P("section", None, None),
        P("section", None, "dp"),
        P("section", "dp", None),
        P("section", None, "dp"),
        P("section", "dp", None),
        P("section", None, None),
        P("section", None),
        P("section", None),
        P("section", None, "dp"),
        P("section", "dp", None),
        P("section", None),
    )
    return jax.shard_map(shards, mesh=mesh, in_specs=in_specs, out_specs=out_specs, check_vma=False)
```
